128 devices in a mesh: dp: 2 (over core), expert: 64 (over y, x, z).
Axes of the slice: x: 4, y: 4, z: 4, core: 2. Of those that a mesh axis runs over, the one named last changes fastest.
Arguments:
- tokens: bfloat16 [16384, 2048], P(('dp', 'expert')), may hold values from -6 to 6
- gates: float32 [16384, 8], P(('dp', 'expert')), may hold values from 0.05 to 0.5
- expert_ids: int32 [16384, 8], P(('dp', 'expert')), may hold values from 0 to 63, as said below
- slots: int32 [16384, 8], P(('dp', 'expert')), may hold values from -1 to 15, as said below
- grad_out: bfloat16 [16384, 2048], P(('dp', 'expert')), may hold values from -6 to 6
- expert_weights: bfloat16 [64, 3, 2048, 768], P('expert', None, None, 'dp'), may hold values from -0.125 to 0.125
Outputs:
- combined: bfloat16 [16384, 2048], P(('dp', 'expert'))
- gate_grads: float32 [16384, 8], P(('dp', 'expert'))
- token_grads: bfloat16 [16384, 2048], P(('dp', 'expert'))
- weight_grads: bfloat16 [64, 3, 2048, 768], P('expert', None, None, 'dp')
The draws below stay inside these ranges and needn't reach their ends.
Inputs may be any that keep to these rules, and one draw needn't show every extreme that they name: `expert_ids`: each token names 8 distinct experts. Within each device block of 128 tokens, the choices are counted in token then choice order for each expert; slots holds that count, or -1 once 16 earlier choices of the block went to that expert.
All inputs are finite; a program needn't handle non-finite values.
Results may differ from the reference program's by a relative error of at most 0.008.
Values may be sent and summed in bfloat16 or wider, within the bound.
A program may use at most 192 MiB of HBM per device.

```python
import jax
import jax.numpy as jnp
from jax import lax

D = 2048
HID = 768
TOP = 8
TOK_DEV = 128
EXPERTS = 64
CAP = 16
TOKENS = 16384
N_DP = 2


def route_pair(key):
    blocks = TOKENS // TOK_DEV
    starting_offset = jax.random.randint(jax.random.fold_in(key, 11), (TOKENS, EXPERTS), 0, 2 ** 14) * EXPERTS
    column_entry = jnp.arange(EXPERTS, dtype=jnp.int32)[None, :]
    starting_offset = starting_offset + column_entry
    shared_onehot_mask = jax.random.randint(jax.random.fold_in(key, 12), (), 0, EXPERTS)
    block_hot = jax.random.randint(jax.random.fold_in(key, 13), (blocks,), 0, EXPERTS)
    coins = jax.random.randint(jax.random.fold_in(key, 14), (TOKENS, 2), 0, 2)
    orders = jax.vmap(lambda sub: jax.random.permutation(sub, TOK_DEV))(jax.random.split(jax.random.fold_in(key, 15), blocks))
    leading_choice = (orders.reshape(-1) < TOK_DEV // 2) | (coins[:, 0] == 1)
    trailing_choice = coins[:, 1] == 1
    owning_block = jnp.repeat(block_hot, TOK_DEV)
    extra_score = jnp.where(leading_choice[:, None] & (column_entry == shared_onehot_mask), 2 ** 21, 0)
    extra_score = extra_score + jnp.where(trailing_choice[:, None] & (column_entry == owning_block[:, None]), 2 ** 21, 0)
    router_scores = (starting_offset + extra_score).astype(jnp.int32)
    unused, chosen = lax.top_k(router_scores, TOP)
    chosen = chosen.astype(jnp.int32)
    onehot = (chosen.reshape(blocks, TOK_DEV * TOP)[:, :, None] == column_entry[None, :, :]).astype(jnp.int32)
    place = jnp.sum(jnp.cumsum(onehot, axis=1) * onehot, axis=2) - 1
    slot_values = jnp.where(place < CAP, place, -1).reshape(TOKENS, TOP).astype(jnp.int32)
    return (chosen, slot_values)


def draw_expert_ids(key, part):
    return route_pair(key)[0]


def draw_slots(key, part):
    return route_pair(key)[1]


def steps_of(key, extent, pieces, least, top_value):
    factor_of = 1.0
    for dim, parts in pieces:
        draws = jax.random.uniform(jax.random.fold_in(jax.random.fold_in(key, 6), dim), (parts,), jnp.float32, least / len(pieces), top_value / len(pieces))
        factor_of = factor_of * jnp.repeat(jnp.exp(draws), extent[dim] // parts).reshape((-1,) + (1,) * (len(extent) - 1 - dim))
    return factor_of


def scatter_about(own_key, dims, scale, bound, cuts=(), kind=jnp.bfloat16):
    drawn = jax.random.normal(own_key, dims, jnp.float32) * scale
    if len(cuts) > 0:
        drawn = steps_of(own_key, dims, cuts, -0.22, 0.18) * drawn
    return jnp.clip(drawn, min=-bound, max=bound).astype(kind)


def setup_inputs(seed: int = 0) -> dict:
    key_of = jax.random.split(jax.random.key(seed), 7)
    return {
        "tokens": scatter_about(key_of[0], (TOKENS, D), 1.0, 6.0, ((0, 128),)),
        "gates": jnp.clip(0.05 + 0.45 * jax.random.uniform(key_of[1], (TOKENS, TOP), jnp.float32) ** steps_of(key_of[1], (TOKENS, TOP), ((0, 128),), -0.2, 0.2), 0.05, 0.5),
        "expert_ids": draw_expert_ids(jax.random.fold_in(key_of[6], 71), 0),
        "slots": draw_slots(jax.random.fold_in(key_of[6], 71), 0),
        "grad_out": scatter_about(key_of[4], (TOKENS, D), 1.0, 6.0, ((0, 128),)),
        "expert_weights": scatter_about(key_of[5], (EXPERTS, 3, D, HID), D ** -0.5, 0.125, ((0, 64), (3, 2))),
    }


def contract_rows(left, right):
    return lax.dot_general(left, right, (((0,), (0,)), ((), ())), preferred_element_type=jnp.float32)


def contract_last(left, right):
    return lax.dot_general(left, right, (((1,), (1,)), ((), ())), preferred_element_type=jnp.float32)


def expert_pass(inputs, grad_rows, weights):
    gate_pre = jnp.dot(inputs, weights[0], preferred_element_type=jnp.float32)
    up_pre = jnp.dot(inputs, weights[1], preferred_element_type=jnp.float32)
    sigmoid_gate = jax.nn.sigmoid(gate_pre)
    activated = (gate_pre * sigmoid_gate * up_pre).astype(jnp.bfloat16)
    expert_out = contract_last(activated, weights[2]).astype(jnp.bfloat16)
    grad_act = jnp.dot(grad_rows, weights[2], preferred_element_type=jnp.float32)
    grad_gate = (grad_act * up_pre * sigmoid_gate * (1.0 + gate_pre * (1.0 - sigmoid_gate))).astype(jnp.bfloat16)
    grad_up = (grad_act * gate_pre * sigmoid_gate).astype(jnp.bfloat16)
    row_grads = (contract_last(grad_gate, weights[0]) + contract_last(grad_up, weights[1])).astype(jnp.bfloat16)
    stacked = jnp.stack([contract_rows(inputs, grad_gate), contract_rows(inputs, grad_up), contract_rows(grad_rows, activated)])
    return expert_out, row_grads, stacked.astype(jnp.bfloat16)


def reference(tokens, gates, expert_ids, slots, grad_out, expert_weights):
    slot_rows = EXPERTS * CAP
    whole = N_DP * EXPERTS * slot_rows
    position = jnp.arange(TOKENS, dtype=jnp.int32)
    replica = position // (TOK_DEV * EXPERTS)
    source = (position // TOK_DEV) % EXPERTS
    target = jnp.where(slots >= 0, ((expert_ids * N_DP + replica[:, None]) * EXPERTS + source[:, None]) * CAP + slots, whole).astype(jnp.int32)
    anchor = jnp.broadcast_to(position[:, None], (TOKENS, TOP)).astype(jnp.int32)
    holder = jnp.full((whole,), TOKENS, jnp.int32).at[target.reshape(-1)].set(anchor.reshape(-1), mode="drop")
    holder = holder.reshape(EXPERTS, N_DP * slot_rows)
    slot_gate = jnp.zeros((whole,), jnp.float32).at[target.reshape(-1)].set(gates.reshape(-1), mode="drop")
    slot_gate = slot_gate.reshape(EXPERTS, N_DP * slot_rows)
    padding = jnp.zeros((1, D), jnp.bfloat16)
    token_table = jnp.concatenate([tokens, padding], 0)
    grad_table = jnp.concatenate([grad_out, padding], 0)

    def per_expert(index):
        chosen = holder[index]
        inputs = token_table[chosen]
        grad_rows = (slot_gate[index][:, None] * grad_table[chosen].astype(jnp.float32)).astype(jnp.bfloat16)
        return expert_pass(inputs, grad_rows, expert_weights[index])

    expert_out, row_grads, weight_grads = lax.map(per_expert, jnp.arange(EXPERTS, dtype=jnp.int32))
    out_table = jnp.concatenate([expert_out.reshape(-1, D), padding], 0)
    back_table = jnp.concatenate([row_grads.reshape(-1, D), padding], 0)
    combined = jnp.zeros((TOKENS, D), jnp.float32)
    token_grads = jnp.zeros((TOKENS, D), jnp.float32)
    gate_cols = []
    for choice_index in range(TOP):
        picked = out_table[target[:, choice_index]].astype(jnp.float32)
        combined = combined + gates[:, choice_index:choice_index + 1] * picked
        gate_cols.append(jnp.sum(grad_out.astype(jnp.float32) * picked, axis=1))
        token_grads = token_grads + back_table[target[:, choice_index]].astype(jnp.float32)
    gate_grads = jnp.stack(gate_cols, axis=1)
    return combined.astype(jnp.bfloat16), gate_grads, token_grads.astype(jnp.bfloat16), weight_grads
```

```python
import jax
import jax.numpy as jnp
from jax import lax
from jax.sharding import PartitionSpec as P


def contract_rows(left, right):
    return lax.dot_general(
        left, right, (((0,), (0,)), ((), ())), preferred_element_type=jnp.float32
    )


def contract_last(left, right):
    return lax.dot_general(
        left, right, (((1,), (1,)), ((), ())), preferred_element_type=jnp.float32
    )


def split3(x):
    hi = x.astype(jnp.bfloat16)
    rest = x - hi.astype(jnp.float32)
    mid = rest.astype(jnp.bfloat16)
    lo = (rest - mid.astype(jnp.float32)).astype(jnp.bfloat16)
    return hi, mid, lo


def scaled_rows(weights, rows):
    hi, mid, lo = split3(weights)
    dot = lambda w: jnp.dot(w, rows, preferred_element_type=jnp.float32)
    return dot(hi) + dot(mid) + dot(lo)


def scaled_cols(weights, rows):
    hi, mid, lo = split3(weights)
    return contract_rows(hi, rows) + contract_rows(mid, rows) + contract_rows(lo, rows)


def local(tokens, gates, expert_ids, slots, grad_out, expert_weights):
    n_expert = lax.axis_size("expert")
    tok_count, top_count = expert_ids.shape
    capacity = tok_count * top_count // n_expert
    slot_rows = n_expert * capacity
    target = jnp.where(slots >= 0, expert_ids * capacity + slots, slot_rows)
    slot_ids = jnp.arange(slot_rows, dtype=jnp.int32)
    hit = target[:, :, None] == slot_ids[None, None, :]
    select = jnp.sum(hit.astype(jnp.float32), axis=1)
    slot_gate = jnp.sum(jnp.where(hit, gates[:, :, None], 0.0), axis=1)
    select_bf = select.astype(jnp.bfloat16)
    send_tokens = contract_rows(select_bf, tokens).astype(jnp.bfloat16)
    send_grads = scaled_cols(slot_gate, grad_out).astype(jnp.bfloat16)
    arrived_tokens = lax.all_to_all(send_tokens, "expert", split_axis=0, concat_axis=0, tiled=True)
    arrived_tokens, send_grads = lax.optimization_barrier((arrived_tokens, send_grads))
    arrived_grads = lax.all_to_all(send_grads, "expert", split_axis=0, concat_axis=0, tiled=True)
    weights = lax.all_gather(expert_weights, "dp", axis=3, tiled=True)[0]
    inputs = arrived_tokens
    gate_pre = jnp.dot(inputs, weights[0], preferred_element_type=jnp.float32)
    up_pre = jnp.dot(inputs, weights[1], preferred_element_type=jnp.float32)
    sigmoid_gate = jax.nn.sigmoid(gate_pre)
    activated = (gate_pre * sigmoid_gate * up_pre).astype(jnp.bfloat16)
    summand = contract_last(activated, weights[2])
    results = summand.astype(jnp.bfloat16)
    results, arrived_grads = lax.optimization_barrier((results, arrived_grads))
    back_out = lax.all_to_all(results, "expert", split_axis=0, concat_axis=0, tiled=True)
    grad_act = jnp.dot(arrived_grads, weights[2], preferred_element_type=jnp.float32)
    grad_gate = (grad_act * up_pre * sigmoid_gate * (1.0 + gate_pre * (1.0 - sigmoid_gate))).astype(
        jnp.bfloat16
    )
    grad_up = (grad_act * gate_pre * sigmoid_gate).astype(jnp.bfloat16)
    summand = contract_last(grad_gate, weights[0]) + contract_last(grad_up, weights[1])
    row_grads = summand.astype(jnp.bfloat16)
    row_grads, back_out, inputs, grad_gate, grad_up, arrived_grads, activated = (
        lax.optimization_barrier(
            (row_grads, back_out, inputs, grad_gate, grad_up, arrived_grads, activated)
        )
    )
    weight_grads = jnp.stack(
        [
            lax.psum_scatter(
                contract_rows(left, right)[None], "dp", scatter_dimension=2, tiled=True
            ).astype(jnp.bfloat16)
            for left, right in (
                (inputs, grad_gate),
                (inputs, grad_up),
                (arrived_grads, activated),
            )
        ],
        axis=1,
    )
    back_grads = lax.all_to_all(row_grads, "expert", split_axis=0, concat_axis=0, tiled=True)
    combined = scaled_rows(slot_gate, back_out).astype(jnp.bfloat16)
    products = contract_last(grad_out, back_out)
    gate_grads = jnp.sum(jnp.where(hit, products[:, None, :], 0.0), axis=2)
    token_grads = jnp.dot(select_bf, back_grads, preferred_element_type=jnp.float32).astype(
        jnp.bfloat16
    )
    return (combined, gate_grads, token_grads, weight_grads)


def solution(mesh):
    placed = (
        P(("dp", "expert"), None),
        P(("dp", "expert"), None),
        P(("dp", "expert"), None),
        P(("dp", "expert"), None),
        P(("dp", "expert"), None),
        P("expert", None, None, "dp"),
    )
    return jax.shard_map(
        local,
        mesh=mesh,
        in_specs=placed,
        out_specs=(
            P(("dp", "expert"), None),
            P(("dp", "expert"), None),
            P(("dp", "expert"), None),
            P("expert", None, None, "dp"),
        ),
        check_vma=False,
    )
```

```python
import jax
import jax.numpy as jnp
from jax import lax
from jax.sharding import PartitionSpec as P


def contract_rows(left, right):
    return lax.dot_general(
        left, right, (((0,), (0,)), ((), ())), preferred_element_type=jnp.float32
    )


def contract_last(left, right):
    return lax.dot_general(
        left, right, (((1,), (1,)), ((), ())), preferred_element_type=jnp.float32
    )


def split3(x):
    hi = x.astype(jnp.bfloat16)
    rest = x - hi.astype(jnp.float32)
    mid = rest.astype(jnp.bfloat16)
    lo = (rest - mid.astype(jnp.float32)).astype(jnp.bfloat16)
    return hi, mid, lo


def scaled_rows(weights, rows):
    hi, mid, lo = split3(weights)
    dot = lambda w: jnp.dot(w, rows, preferred_element_type=jnp.float32)
    return dot(hi) + dot(mid) + dot(lo)


def scaled_cols(weights, rows):
    hi, mid, lo = split3(weights)
    return contract_rows(hi, rows) + contract_rows(mid, rows) + contract_rows(lo, rows)


def local(tokens, gates, expert_ids, slots, grad_out, expert_weights):
    n_expert = lax.axis_size("expert")
    tok_count, top_count = expert_ids.shape
    capacity = tok_count * top_count // n_expert
    slot_rows = n_expert * capacity
    target = jnp.where(slots >= 0, expert_ids * capacity + slots, slot_rows)
    slot_ids = jnp.arange(slot_rows, dtype=jnp.int32)
    hit = target[:, :, None] == slot_ids[None, None, :]
    select = jnp.sum(hit.astype(jnp.float32), axis=1)
    slot_gate = jnp.sum(jnp.where(hit, gates[:, :, None], 0.0), axis=1)
    select_bf = select.astype(jnp.bfloat16)
    send_tokens = contract_rows(select_bf, tokens).astype(jnp.bfloat16)
    send_grads = scaled_cols(slot_gate, grad_out).astype(jnp.bfloat16)
    arrived_tokens = lax.all_to_all(send_tokens, "expert", split_axis=0, concat_axis=0, tiled=True)
    arrived_tokens, send_grads = lax.optimization_barrier((arrived_tokens, send_grads))
    arrived_grads = lax.all_to_all(send_grads, "expert", split_axis=0, concat_axis=0, tiled=True)
    weights = lax.all_gather(expert_weights, "dp", axis=3, tiled=True)[0]
    inputs = arrived_tokens
    gate_pre = jnp.dot(inputs, weights[0], preferred_element_type=jnp.float32)
    up_pre = jnp.dot(inputs, weights[1], preferred_element_type=jnp.float32)
    sigmoid_gate = jax.nn.sigmoid(gate_pre)
    activated = (gate_pre * sigmoid_gate * up_pre).astype(jnp.bfloat16)
    summand = contract_last(activated, weights[2])
    results = summand.astype(jnp.bfloat16)
    results, arrived_grads = lax.optimization_barrier((results, arrived_grads))
    back_out = lax.all_to_all(results, "expert", split_axis=0, concat_axis=0, tiled=True)
    grad_act = jnp.dot(arrived_grads, weights[2], preferred_element_type=jnp.float32)
    grad_gate = (grad_act * up_pre * sigmoid_gate * (1.0 + gate_pre * (1.0 - sigmoid_gate))).astype(
        jnp.bfloat16
    )
    grad_up = (grad_act * gate_pre * sigmoid_gate).astype(jnp.bfloat16)
    summand = contract_last(grad_gate, weights[0]) + contract_last(grad_up, weights[1])
    row_grads = summand.astype(jnp.bfloat16)
    row_grads, back_out, inputs, grad_gate, grad_up, arrived_grads, activated = (
        lax.optimization_barrier(
            (row_grads, back_out, inputs, grad_gate, grad_up, arrived_grads, activated)
        )
    )
    half = grad_gate.shape[1] // 2
    gate_up = jnp.concatenate(
        [grad_gate[:, :half], grad_up[:, :half], grad_gate[:, half:], grad_up[:, half:]], 1
    )
    gate_up_grads = lax.psum_scatter(
        contract_rows(inputs, gate_up), "dp", scatter_dimension=1, tiled=True
    )
    down_grads = lax.psum_scatter(
        contract_rows(arrived_grads, activated), "dp", scatter_dimension=1, tiled=True
    )
    weight_grads = jnp.stack(
        [gate_up_grads[:, :half], gate_up_grads[:, half:], down_grads]
    )[None].astype(jnp.bfloat16)
    back_grads = lax.all_to_all(row_grads, "expert", split_axis=0, concat_axis=0, tiled=True)
    combined = scaled_rows(slot_gate, back_out).astype(jnp.bfloat16)
    products = contract_last(grad_out, back_out)
    gate_grads = jnp.sum(jnp.where(hit, products[:, None, :], 0.0), axis=2)
    token_grads = jnp.dot(select_bf, back_grads, preferred_element_type=jnp.float32).astype(
        jnp.bfloat16
    )
    return (combined, gate_grads, token_grads, weight_grads)


def solution(mesh):
    placed = (
        P(("dp", "expert"), None),
        P(("dp", "expert"), None),
        P(("dp", "expert"), None),
        P(("dp", "expert"), None),
        P(("dp", "expert"), None),
        P("expert", None, None, "dp"),
    )
    return jax.shard_map(
        local,
        mesh=mesh,
        in_specs=placed,
        out_specs=(
            P(("dp", "expert"), None),
            P(("dp", "expert"), None),
            P(("dp", "expert"), None),
            P("expert", None, None, "dp"),
        ),
        check_vma=False,
    )
```

```python
import jax
import jax.numpy as jnp
from jax import lax
from jax.sharding import PartitionSpec as P


def contract_rows(left, right):
    return lax.dot_general(
        left, right, (((0,), (0,)), ((), ())), preferred_element_type=jnp.float32
    )


def contract_last(left, right):
    return lax.dot_general(
        left, right, (((1,), (1,)), ((), ())), preferred_element_type=jnp.float32
    )


def split3(x):
    hi = x.astype(jnp.bfloat16)
    rest = x - hi.astype(jnp.float32)
    mid = rest.astype(jnp.bfloat16)
    lo = (rest - mid.astype(jnp.float32)).astype(jnp.bfloat16)
    return hi, mid, lo


def scaled_rows(weights, rows):
    hi, mid, lo = split3(weights)
    dot = lambda w: jnp.dot(w, rows, preferred_element_type=jnp.float32)
    return dot(hi) + dot(mid) + dot(lo)


def scaled_cols(weights, rows):
    hi, mid, lo = split3(weights)
    return contract_rows(hi, rows) + contract_rows(mid, rows) + contract_rows(lo, rows)


def local(tokens, gates, expert_ids, slots, grad_out, expert_weights):
    n_expert = lax.axis_size("expert")
    tok_count, top_count = expert_ids.shape
    capacity = tok_count * top_count // n_expert
    slot_rows = n_expert * capacity
    target = jnp.where(slots >= 0, expert_ids * capacity + slots, slot_rows)
    slot_ids = jnp.arange(slot_rows, dtype=jnp.int32)
    hit = target[:, :, None] == slot_ids[None, None, :]
    select = jnp.sum(hit.astype(jnp.float32), axis=1)
    slot_gate = jnp.sum(jnp.where(hit, gates[:, :, None], 0.0), axis=1)
    select_bf = select.astype(jnp.bfloat16)
    send_tokens = contract_rows(select_bf, tokens).astype(jnp.bfloat16)
    send_grads = scaled_cols(slot_gate, grad_out).astype(jnp.bfloat16)
    arrived_tokens = lax.all_to_all(send_tokens, "expert", split_axis=0, concat_axis=0, tiled=True)
    arrived_tokens, send_grads = lax.optimization_barrier((arrived_tokens, send_grads))
    arrived_grads = lax.all_to_all(send_grads, "expert", split_axis=0, concat_axis=0, tiled=True)
    weights = lax.all_gather(expert_weights, "dp", axis=3, tiled=True)[0]
    inputs = arrived_tokens
    gate_pre = jnp.dot(inputs, weights[0], preferred_element_type=jnp.float32)
    up_pre = jnp.dot(inputs, weights[1], preferred_element_type=jnp.float32)
    sigmoid_gate = jax.nn.sigmoid(gate_pre)
    activated = (gate_pre * sigmoid_gate * up_pre).astype(jnp.bfloat16)
    summand = contract_last(activated, weights[2])
    results = summand.astype(jnp.bfloat16)
    results, arrived_grads = lax.optimization_barrier((results, arrived_grads))
    back_out = lax.all_to_all(results, "expert", split_axis=0, concat_axis=0, tiled=True)
    grad_act = jnp.dot(arrived_grads, weights[2], preferred_element_type=jnp.float32)
    grad_gate = (grad_act * up_pre * sigmoid_gate * (1.0 + gate_pre * (1.0 - sigmoid_gate))).astype(
        jnp.bfloat16
    )
    grad_up = (grad_act * gate_pre * sigmoid_gate).astype(jnp.bfloat16)
    summand = contract_last(grad_gate, weights[0]) + contract_last(grad_up, weights[1])
    row_grads = summand.astype(jnp.bfloat16)
    half = grad_gate.shape[1] // 2
    gate_up = jnp.concatenate(
        [grad_gate[:, :half], grad_up[:, :half], grad_gate[:, half:], grad_up[:, half:]], 1
    )
    gate_up_grads = contract_rows(inputs, gate_up)
    down_grads = contract_rows(arrived_grads, activated)
    row_grads, back_out, gate_up_grads, down_grads = lax.optimization_barrier(
        (row_grads, back_out, gate_up_grads, down_grads)
    )
    gate_up_grads = lax.psum_scatter(gate_up_grads, "dp", scatter_dimension=1, tiled=True)
    down_grads = lax.psum_scatter(down_grads, "dp", scatter_dimension=1, tiled=True)
    weight_grads = jnp.stack(
        [gate_up_grads[:, :half], gate_up_grads[:, half:], down_grads]
    )[None].astype(jnp.bfloat16)
    back_grads = lax.all_to_all(row_grads, "expert", split_axis=0, concat_axis=0, tiled=True)
    combined = scaled_rows(slot_gate, back_out).astype(jnp.bfloat16)
    products = contract_last(grad_out, back_out)
    gate_grads = jnp.sum(jnp.where(hit, products[:, None, :], 0.0), axis=2)
    token_grads = jnp.dot(select_bf, back_grads, preferred_element_type=jnp.float32).astype(
        jnp.bfloat16
    )
    return (combined, gate_grads, token_grads, weight_grads)


def solution(mesh):
    placed = (
        P(("dp", "expert"), None),
        P(("dp", "expert"), None),
        P(("dp", "expert"), None),
        P(("dp", "expert"), None),
        P(("dp", "expert"), None),
        P("expert", None, None, "dp"),
    )
    return jax.shard_map(
        local,
        mesh=mesh,
        in_specs=placed,
        out_specs=(
            P(("dp", "expert"), None),
            P(("dp", "expert"), None),
            P(("dp", "expert"), None),
            P("expert", None, None, "dp"),
        ),
        check_vma=False,
    )
```

```python
import jax
import jax.numpy as jnp
from jax import lax
from jax.sharding import PartitionSpec as P


def contract_rows(left, right):
    return lax.dot_general(
        left, right, (((0,), (0,)), ((), ())), preferred_element_type=jnp.float32
    )


def contract_last(left, right):
    return lax.dot_general(
        left, right, (((1,), (1,)), ((), ())), preferred_element_type=jnp.float32
    )


def split3(x):
    hi = x.astype(jnp.bfloat16)
    rest = x - hi.astype(jnp.float32)
    mid = rest.astype(jnp.bfloat16)
    lo = (rest - mid.astype(jnp.float32)).astype(jnp.bfloat16)
    return hi, mid, lo


def scaled_rows(weights, rows):
    hi, mid, lo = split3(weights)
    dot = lambda w: jnp.dot(w, rows, preferred_element_type=jnp.float32)
    return dot(hi) + dot(mid) + dot(lo)


def scaled_cols(weights, rows):
    hi, mid, lo = split3(weights)
    return contract_rows(hi, rows) + contract_rows(mid, rows) + contract_rows(lo, rows)


def local(tokens, gates, expert_ids, slots, grad_out, expert_weights):
    n_expert = lax.axis_size("expert")
    tok_count, top_count = expert_ids.shape
    capacity = tok_count * top_count // n_expert
    slot_rows = n_expert * capacity
    target = jnp.where(slots >= 0, expert_ids * capacity + slots, slot_rows)
    slot_ids = jnp.arange(slot_rows, dtype=jnp.int32)
    hit = target[:, :, None] == slot_ids[None, None, :]
    select = jnp.sum(hit.astype(jnp.float32), axis=1)
    slot_gate = jnp.sum(jnp.where(hit, gates[:, :, None], 0.0), axis=1)
    select_bf = select.astype(jnp.bfloat16)
    send_tokens = contract_rows(select_bf, tokens).astype(jnp.bfloat16)
    send_grads = scaled_cols(slot_gate, grad_out).astype(jnp.bfloat16)
    arrived_tokens = lax.all_to_all(send_tokens, "expert", split_axis=0, concat_axis=0, tiled=True)
    arrived_tokens, send_grads = lax.optimization_barrier((arrived_tokens, send_grads))
    arrived_grads = lax.all_to_all(send_grads, "expert", split_axis=0, concat_axis=0, tiled=True)
    weights = lax.all_gather(expert_weights, "dp", axis=3, tiled=True)[0]
    inputs = arrived_tokens
    gate_pre = jnp.dot(inputs, weights[0], preferred_element_type=jnp.float32)
    up_pre = jnp.dot(inputs, weights[1], preferred_element_type=jnp.float32)
    sigmoid_gate = jax.nn.sigmoid(gate_pre)
    activated = (gate_pre * sigmoid_gate * up_pre).astype(jnp.bfloat16)
    summand = contract_last(activated, weights[2])
    results = summand.astype(jnp.bfloat16)
    results, arrived_grads = lax.optimization_barrier((results, arrived_grads))
    back_out = lax.all_to_all(results, "expert", split_axis=0, concat_axis=0, tiled=True)
    grad_act = jnp.dot(arrived_grads, weights[2], preferred_element_type=jnp.float32)
    grad_gate = (grad_act * up_pre * sigmoid_gate * (1.0 + gate_pre * (1.0 - sigmoid_gate))).astype(
        jnp.bfloat16
    )
    grad_up = (grad_act * gate_pre * sigmoid_gate).astype(jnp.bfloat16)
    summand = contract_last(grad_gate, weights[0]) + contract_last(grad_up, weights[1])
    row_grads = summand.astype(jnp.bfloat16)
    half = grad_gate.shape[1] // 2
    gate_up = jnp.concatenate(
        [grad_gate[:, :half], grad_up[:, :half], grad_gate[:, half:], grad_up[:, half:]], 1
    )
    gate_up_grads = contract_rows(inputs, gate_up)
    down_grads = contract_rows(arrived_grads, activated)
    row_grads, back_out, gate_up_grads, down_grads = lax.optimization_barrier(
        (row_grads, back_out, gate_up_grads, down_grads)
    )
    gate_up_grads = lax.psum_scatter(gate_up_grads, "dp", scatter_dimension=1, tiled=True)
    down_grads = lax.psum_scatter(down_grads, "dp", scatter_dimension=1, tiled=True)
    rows = gate_up_grads.shape[0]
    weight_grads = jnp.concatenate(
        [gate_up_grads.reshape(rows, 2, half).transpose(1, 0, 2), down_grads[None]], 0
    )[None].astype(jnp.bfloat16)
    back_grads = lax.all_to_all(row_grads, "expert", split_axis=0, concat_axis=0, tiled=True)
    back_grads, weight_grads = lax.optimization_barrier((back_grads, weight_grads))
    combined = scaled_rows(slot_gate, back_out).astype(jnp.bfloat16)
    products = contract_last(grad_out, back_out)
    gate_grads = jnp.sum(jnp.where(hit, products[:, None, :], 0.0), axis=2)
    token_grads = jnp.dot(select_bf, back_grads, preferred_element_type=jnp.float32).astype(
        jnp.bfloat16
    )
    return (combined, gate_grads, token_grads, weight_grads)


def solution(mesh):
    placed = (
        P(("dp", "expert"), None),
        P(("dp", "expert"), None),
        P(("dp", "expert"), None),
        P(("dp", "expert"), None),
        P(("dp", "expert"), None),
        P("expert", None, None, "dp"),
    )
    return jax.shard_map(
        local,
        mesh=mesh,
        in_specs=placed,
        out_specs=(
            P(("dp", "expert"), None),
            P(("dp", "expert"), None),
            P(("dp", "expert"), None),
            P("expert", None, None, "dp"),
        ),
        check_vma=False,
    )
```

```python
import jax
import jax.numpy as jnp
from jax import lax
from jax.sharding import PartitionSpec as P


def contract_rows(left, right):
    return lax.dot_general(
        left, right, (((0,), (0,)), ((), ())), preferred_element_type=jnp.float32
    )


def contract_last(left, right):
    return lax.dot_general(
        left, right, (((1,), (1,)), ((), ())), preferred_element_type=jnp.float32
    )


def split3(x):
    hi = x.astype(jnp.bfloat16)
    rest = x - hi.astype(jnp.float32)
    mid = rest.astype(jnp.bfloat16)
    lo = (rest - mid.astype(jnp.float32)).astype(jnp.bfloat16)
    return hi, mid, lo


def scaled_rows(weights, rows):
    hi, mid, lo = split3(weights)
    dot = lambda w: jnp.dot(w, rows, preferred_element_type=jnp.float32)
    return dot(hi) + dot(mid) + dot(lo)


def scaled_cols(weights, rows):
    hi, mid, lo = split3(weights)
    return contract_rows(hi, rows) + contract_rows(mid, rows) + contract_rows(lo, rows)


def local(tokens, gates, expert_ids, slots, grad_out, expert_weights):
    n_expert = lax.axis_size("expert")
    tok_count, top_count = expert_ids.shape
    capacity = tok_count * top_count // n_expert
    slot_rows = n_expert * capacity
    target = jnp.where(slots >= 0, expert_ids * capacity + slots, slot_rows)
    slot_ids = jnp.arange(slot_rows, dtype=jnp.int32)
    hit = target[:, :, None] == slot_ids[None, None, :]
    select = jnp.sum(hit.astype(jnp.float32), axis=1)
    slot_gate = jnp.sum(jnp.where(hit, gates[:, :, None], 0.0), axis=1)
    select_bf = select.astype(jnp.bfloat16)
    send_tokens = contract_rows(select_bf, tokens).astype(jnp.bfloat16)
    send_grads = scaled_cols(slot_gate, grad_out).astype(jnp.bfloat16)
    arrived_tokens = lax.all_to_all(send_tokens, "expert", split_axis=0, concat_axis=0, tiled=True)
    arrived_tokens, send_grads = lax.optimization_barrier((arrived_tokens, send_grads))
    arrived_grads = lax.all_to_all(send_grads, "expert", split_axis=0, concat_axis=0, tiled=True)
    weights = lax.all_gather(expert_weights, "dp", axis=3, tiled=True)[0]
    half = expert_weights.shape[3]
    gate_up_weights = jnp.concatenate(
        [weights[0, :, :half], weights[1, :, :half], weights[0, :, half:], weights[1, :, half:]], 1
    )
    down_weights = weights[2]
    inputs = arrived_tokens
    rows = inputs.shape[0]
    both_pre = jnp.dot(inputs, gate_up_weights, preferred_element_type=jnp.float32).reshape(
        rows, 2, 2, half
    )
    gate_pre = both_pre[:, :, 0].reshape(rows, 2 * half)
    up_pre = both_pre[:, :, 1].reshape(rows, 2 * half)
    sigmoid_gate = jax.nn.sigmoid(gate_pre)
    activated = (gate_pre * sigmoid_gate * up_pre).astype(jnp.bfloat16)
    summand = contract_last(activated, down_weights)
    results = summand.astype(jnp.bfloat16)
    results, arrived_grads = lax.optimization_barrier((results, arrived_grads))
    back_out = lax.all_to_all(results, "expert", split_axis=0, concat_axis=0, tiled=True)
    grad_act = jnp.dot(arrived_grads, down_weights, preferred_element_type=jnp.float32)
    grad_gate = (grad_act * up_pre * sigmoid_gate * (1.0 + gate_pre * (1.0 - sigmoid_gate))).astype(
        jnp.bfloat16
    )
    grad_up = (grad_act * gate_pre * sigmoid_gate).astype(jnp.bfloat16)
    gate_up = jnp.stack(
        [grad_gate.reshape(rows, 2, half), grad_up.reshape(rows, 2, half)], 2
    ).reshape(rows, 4 * half)
    row_grads = contract_last(gate_up, gate_up_weights).astype(jnp.bfloat16)
    gate_up_grads = contract_rows(inputs, gate_up)
    down_grads = contract_rows(arrived_grads, activated)
    row_grads, back_out, gate_up_grads, down_grads = lax.optimization_barrier(
        (row_grads, back_out, gate_up_grads, down_grads)
    )
    gate_up_grads = lax.psum_scatter(gate_up_grads, "dp", scatter_dimension=1, tiled=True)
    down_grads = lax.psum_scatter(down_grads, "dp", scatter_dimension=1, tiled=True)
    width = gate_up_grads.shape[0]
    weight_grads = jnp.concatenate(
        [gate_up_grads.reshape(width, 2, half).transpose(1, 0, 2), down_grads[None]], 0
    )[None].astype(jnp.bfloat16)
    back_grads = lax.all_to_all(row_grads, "expert", split_axis=0, concat_axis=0, tiled=True)
    back_grads, weight_grads = lax.optimization_barrier((back_grads, weight_grads))
    combined = scaled_rows(slot_gate, back_out).astype(jnp.bfloat16)
    products = contract_last(grad_out, back_out)
    gate_grads = jnp.sum(jnp.where(hit, products[:, None, :], 0.0), axis=2)
    token_grads = jnp.dot(select_bf, back_grads, preferred_element_type=jnp.float32).astype(
        jnp.bfloat16
    )
    return (combined, gate_grads, token_grads, weight_grads)


def solution(mesh):
    placed = (
        P(("dp", "expert"), None),
        P(("dp", "expert"), None),
        P(("dp", "expert"), None),
        P(("dp", "expert"), None),
        P(("dp", "expert"), None),
        P("expert", None, None, "dp"),
    )
    return jax.shard_map(
        local,
        mesh=mesh,
        in_specs=placed,
        out_specs=(
            P(("dp", "expert"), None),
            P(("dp", "expert"), None),
            P(("dp", "expert"), None),
            P("expert", None, None, "dp"),
        ),
        check_vma=False,
    )
```

```python
import jax
import jax.numpy as jnp
from jax import lax
from jax.sharding import PartitionSpec as P


def contract_rows(left, right):
    return lax.dot_general(
        left, right, (((0,), (0,)), ((), ())), preferred_element_type=jnp.float32
    )


def contract_last(left, right):
    return lax.dot_general(
        left, right, (((1,), (1,)), ((), ())), preferred_element_type=jnp.float32
    )


def split3(x):
    hi = x.astype(jnp.bfloat16)
    rest = x - hi.astype(jnp.float32)
    mid = rest.astype(jnp.bfloat16)
    lo = (rest - mid.astype(jnp.float32)).astype(jnp.bfloat16)
    return hi, mid, lo


def scaled_rows(weights, rows):
    hi, mid, lo = split3(weights)
    dot = lambda w: jnp.dot(w, rows, preferred_element_type=jnp.float32)
    return dot(hi) + dot(mid) + dot(lo)


def scaled_cols(weights, rows):
    hi, mid, lo = split3(weights)
    return contract_rows(hi, rows) + contract_rows(mid, rows) + contract_rows(lo, rows)


def local(tokens, gates, expert_ids, slots, grad_out, expert_weights):
    n_expert = lax.axis_size("expert")
    tok_count, top_count = expert_ids.shape
    capacity = tok_count * top_count // n_expert
    slot_rows = n_expert * capacity
    target = jnp.where(slots >= 0, expert_ids * capacity + slots, slot_rows)
    slot_ids = jnp.arange(slot_rows, dtype=jnp.int32)
    hit = target[:, :, None] == slot_ids[None, None, :]
    select = jnp.sum(hit.astype(jnp.float32), axis=1)
    slot_gate = jnp.sum(jnp.where(hit, gates[:, :, None], 0.0), axis=1)
    select_bf = select.astype(jnp.bfloat16)
    send_tokens = contract_rows(select_bf, tokens).astype(jnp.bfloat16)
    send_grads = scaled_cols(slot_gate, grad_out).astype(jnp.bfloat16)
    weights = lax.all_gather(expert_weights, "dp", axis=3, tiled=True)[0]
    half = expert_weights.shape[3]
    gate_up_weights = jnp.concatenate(
        [weights[0, :, :half], weights[1, :, :half], weights[0, :, half:], weights[1, :, half:]], 1
    )
    down_weights = weights[2]
    arrived_tokens = lax.all_to_all(send_tokens, "expert", split_axis=0, concat_axis=0, tiled=True)
    arrived_tokens, send_grads, gate_up_weights = lax.optimization_barrier(
        (arrived_tokens, send_grads, gate_up_weights)
    )
    arrived_grads = lax.all_to_all(send_grads, "expert", split_axis=0, concat_axis=0, tiled=True)
    inputs = arrived_tokens
    rows = inputs.shape[0]
    gate_pre = jnp.dot(inputs, weights[0], preferred_element_type=jnp.float32)
    up_pre = jnp.dot(inputs, weights[1], preferred_element_type=jnp.float32)
    sigmoid_gate = jax.nn.sigmoid(gate_pre)
    activated = (gate_pre * sigmoid_gate * up_pre).astype(jnp.bfloat16)
    summand = contract_last(activated, down_weights)
    results = summand.astype(jnp.bfloat16)
    results, arrived_grads = lax.optimization_barrier((results, arrived_grads))
    back_out = lax.all_to_all(results, "expert", split_axis=0, concat_axis=0, tiled=True)
    grad_act = jnp.dot(arrived_grads, down_weights, preferred_element_type=jnp.float32)
    grad_gate = (grad_act * up_pre * sigmoid_gate * (1.0 + gate_pre * (1.0 - sigmoid_gate))).astype(
        jnp.bfloat16
    )
    grad_up = (grad_act * gate_pre * sigmoid_gate).astype(jnp.bfloat16)
    gate_up = jnp.stack(
        [grad_gate.reshape(rows, 2, half), grad_up.reshape(rows, 2, half)], 2
    ).reshape(rows, 4 * half)
    row_grads = contract_last(gate_up, gate_up_weights).astype(jnp.bfloat16)
    gate_up_grads = contract_rows(inputs, gate_up)
    down_grads = contract_rows(arrived_grads, activated)
    row_grads, back_out, gate_up_grads, down_grads = lax.optimization_barrier(
        (row_grads, back_out, gate_up_grads, down_grads)
    )
    gate_up_grads = lax.psum_scatter(gate_up_grads, "dp", scatter_dimension=1, tiled=True)
    down_grads = lax.psum_scatter(down_grads, "dp", scatter_dimension=1, tiled=True)
    width = gate_up_grads.shape[0]
    weight_grads = jnp.concatenate(
        [gate_up_grads.reshape(width, 2, half).transpose(1, 0, 2), down_grads[None]], 0
    )[None].astype(jnp.bfloat16)
    back_grads = lax.all_to_all(row_grads, "expert", split_axis=0, concat_axis=0, tiled=True)
    back_grads, weight_grads = lax.optimization_barrier((back_grads, weight_grads))
    combined = scaled_rows(slot_gate, back_out).astype(jnp.bfloat16)
    products = contract_last(grad_out, back_out)
    gate_grads = jnp.sum(jnp.where(hit, products[:, None, :], 0.0), axis=2)
    token_grads = jnp.dot(select_bf, back_grads, preferred_element_type=jnp.float32).astype(
        jnp.bfloat16
    )
    return (combined, gate_grads, token_grads, weight_grads)


def solution(mesh):
    placed = (
        P(("dp", "expert"), None),
        P(("dp", "expert"), None),
        P(("dp", "expert"), None),
        P(("dp", "expert"), None),
        P(("dp", "expert"), None),
        P("expert", None, None, "dp"),
    )
    return jax.shard_map(
        local,
        mesh=mesh,
        in_specs=placed,
        out_specs=(
            P(("dp", "expert"), None),
            P(("dp", "expert"), None),
            P(("dp", "expert"), None),
            P("expert", None, None, "dp"),
        ),
        check_vma=False,
    )
```

```python
import jax
import jax.numpy as jnp
from jax import lax
from jax.sharding import PartitionSpec as P


def contract_rows(left, right):
    return lax.dot_general(
        left, right, (((0,), (0,)), ((), ())), preferred_element_type=jnp.float32
    )


def contract_last(left, right):
    return lax.dot_general(
        left, right, (((1,), (1,)), ((), ())), preferred_element_type=jnp.float32
    )


def split3(x):
    hi = x.astype(jnp.bfloat16)
    rest = x - hi.astype(jnp.float32)
    mid = rest.astype(jnp.bfloat16)
    lo = (rest - mid.astype(jnp.float32)).astype(jnp.bfloat16)
    return hi, mid, lo


def scaled_rows(weights, rows):
    hi, mid, lo = split3(weights)
    dot = lambda w: jnp.dot(w, rows, preferred_element_type=jnp.float32)
    return dot(hi) + dot(mid) + dot(lo)


def scaled_cols(weights, rows):
    hi, mid, lo = split3(weights)
    return contract_rows(hi, rows) + contract_rows(mid, rows) + contract_rows(lo, rows)


def local(tokens, gates, expert_ids, slots, grad_out, expert_weights):
    n_expert = lax.axis_size("expert")
    tok_count, top_count = expert_ids.shape
    capacity = tok_count * top_count // n_expert
    slot_rows = n_expert * capacity
    target = jnp.where(slots >= 0, expert_ids * capacity + slots, slot_rows)
    slot_ids = jnp.arange(slot_rows, dtype=jnp.int32)
    hit = target[:, :, None] == slot_ids[None, None, :]
    select = jnp.sum(hit.astype(jnp.float32), axis=1)
    slot_gate = jnp.sum(jnp.where(hit, gates[:, :, None], 0.0), axis=1)
    select_bf = select.astype(jnp.bfloat16)
    select_slots = sum(
        (target[:, k][None, :] == slot_ids[:, None]).astype(jnp.float32) for k in range(top_count)
    ).astype(jnp.bfloat16)
    send_tokens = jnp.dot(select_slots, tokens, preferred_element_type=jnp.float32).astype(
        jnp.bfloat16
    )
    send_grads = scaled_cols(slot_gate, grad_out).astype(jnp.bfloat16)
    weights = lax.all_gather(expert_weights, "dp", axis=3, tiled=True)[0]
    half = expert_weights.shape[3]
    gate_up_weights = jnp.concatenate(
        [weights[0, :, :half], weights[1, :, :half], weights[0, :, half:], weights[1, :, half:]], 1
    )
    down_weights = weights[2]
    arrived_tokens = lax.all_to_all(send_tokens, "expert", split_axis=0, concat_axis=0, tiled=True)
    arrived_tokens, send_grads, gate_up_weights = lax.optimization_barrier(
        (arrived_tokens, send_grads, gate_up_weights)
    )
    arrived_grads = lax.all_to_all(send_grads, "expert", split_axis=0, concat_axis=0, tiled=True)
    inputs = arrived_tokens
    rows = inputs.shape[0]
    gate_pre = jnp.dot(inputs, weights[0], preferred_element_type=jnp.float32)
    up_pre = jnp.dot(inputs, weights[1], preferred_element_type=jnp.float32)
    sigmoid_gate = jax.nn.sigmoid(gate_pre)
    activated = (gate_pre * sigmoid_gate * up_pre).astype(jnp.bfloat16)
    summand = contract_last(activated, down_weights)
    results = summand.astype(jnp.bfloat16)
    results, arrived_grads = lax.optimization_barrier((results, arrived_grads))
    back_out = lax.all_to_all(results, "expert", split_axis=0, concat_axis=0, tiled=True)
    grad_act = jnp.dot(arrived_grads, down_weights, preferred_element_type=jnp.float32)
    grad_gate = (grad_act * up_pre * sigmoid_gate * (1.0 + gate_pre * (1.0 - sigmoid_gate))).astype(
        jnp.bfloat16
    )
    grad_up = (grad_act * gate_pre * sigmoid_gate).astype(jnp.bfloat16)
    gate_up = jnp.stack(
        [grad_gate.reshape(rows, 2, half), grad_up.reshape(rows, 2, half)], 2
    ).reshape(rows, 4 * half)
    row_grads = contract_last(gate_up, gate_up_weights).astype(jnp.bfloat16)
    gate_up_grads = contract_rows(inputs, gate_up)
    down_grads = contract_rows(arrived_grads, activated)
    row_grads, back_out, gate_up_grads, down_grads = lax.optimization_barrier(
        (row_grads, back_out, gate_up_grads, down_grads)
    )
    gate_up_grads = lax.psum_scatter(gate_up_grads, "dp", scatter_dimension=1, tiled=True)
    down_grads = lax.psum_scatter(down_grads, "dp", scatter_dimension=1, tiled=True)
    width = gate_up_grads.shape[0]
    weight_grads = jnp.concatenate(
        [gate_up_grads.reshape(width, 2, half).transpose(1, 0, 2), down_grads[None]], 0
    )[None].astype(jnp.bfloat16)
    back_grads = lax.all_to_all(row_grads, "expert", split_axis=0, concat_axis=0, tiled=True)
    back_grads, weight_grads = lax.optimization_barrier((back_grads, weight_grads))
    combined = scaled_rows(slot_gate, back_out).astype(jnp.bfloat16)
    products = contract_last(grad_out, back_out)
    gate_grads = jnp.sum(jnp.where(hit, products[:, None, :], 0.0), axis=2)
    token_grads = contract_rows(back_grads, select_slots).T.astype(jnp.bfloat16)
    return (combined, gate_grads, token_grads, weight_grads)


def solution(mesh):
    placed = (
        P(("dp", "expert"), None),
        P(("dp", "expert"), None),
        P(("dp", "expert"), None),
        P(("dp", "expert"), None),
        P(("dp", "expert"), None),
        P("expert", None, None, "dp"),
    )
    return jax.shard_map(
        local,
        mesh=mesh,
        in_specs=placed,
        out_specs=(
            P(("dp", "expert"), None),
            P(("dp", "expert"), None),
            P(("dp", "expert"), None),
            P("expert", None, None, "dp"),
        ),
        check_vma=False,
    )
```

```python
import jax
import jax.numpy as jnp
from jax import lax
from jax.sharding import PartitionSpec as P


def contract_rows(left, right):
    return lax.dot_general(
        left, right, (((0,), (0,)), ((), ())), preferred_element_type=jnp.float32
    )


def contract_last(left, right):
    return lax.dot_general(
        left, right, (((1,), (1,)), ((), ())), preferred_element_type=jnp.float32
    )


def split3(x):
    hi = x.astype(jnp.bfloat16)
    rest = x - hi.astype(jnp.float32)
    mid = rest.astype(jnp.bfloat16)
    lo = (rest - mid.astype(jnp.float32)).astype(jnp.bfloat16)
    return hi, mid, lo


def scaled_rows(weights, rows):
    hi, mid, lo = split3(weights)
    dot = lambda w: jnp.dot(w, rows, preferred_element_type=jnp.float32)
    return dot(hi) + dot(mid) + dot(lo)


def scaled_cols(weights, rows):
    hi, mid, lo = split3(weights)
    return contract_rows(hi, rows) + contract_rows(mid, rows) + contract_rows(lo, rows)


def local(tokens, gates, expert_ids, slots, grad_out, expert_weights):
    n_expert = lax.axis_size("expert")
    tok_count, top_count = expert_ids.shape
    capacity = tok_count * top_count // n_expert
    slot_rows = n_expert * capacity
    target = jnp.where(slots >= 0, expert_ids * capacity + slots, slot_rows)
    slot_ids = jnp.arange(slot_rows, dtype=jnp.int32)
    hit = target[:, :, None] == slot_ids[None, None, :]
    select = jnp.sum(hit.astype(jnp.float32), axis=1)
    slot_gate = jnp.sum(jnp.where(hit, gates[:, :, None], 0.0), axis=1)
    select_bf = select.astype(jnp.bfloat16)
    select_slots = sum(
        (target[:, k][None, :] == slot_ids[:, None]).astype(jnp.float32) for k in range(top_count)
    ).astype(jnp.bfloat16)
    send_tokens = jnp.dot(select_slots, tokens, preferred_element_type=jnp.float32).astype(
        jnp.bfloat16
    )
    send_grads = scaled_cols(slot_gate, grad_out).astype(jnp.bfloat16)
    arrived_tokens = lax.all_to_all(send_tokens, "expert", split_axis=0, concat_axis=0, tiled=True)
    arrived_tokens, send_grads, expert_weights = lax.optimization_barrier(
        (arrived_tokens, send_grads, expert_weights)
    )
    arrived_grads = lax.all_to_all(send_grads, "expert", split_axis=0, concat_axis=0, tiled=True)
    weights = lax.all_gather(expert_weights, "dp", axis=3, tiled=True)[0]
    half = expert_weights.shape[3]
    gate_up_weights = jnp.concatenate(
        [weights[0, :, :half], weights[1, :, :half], weights[0, :, half:], weights[1, :, half:]], 1
    )
    down_weights = weights[2]
    inputs = arrived_tokens
    rows = inputs.shape[0]
    gate_pre = jnp.dot(inputs, weights[0], preferred_element_type=jnp.float32)
    up_pre = jnp.dot(inputs, weights[1], preferred_element_type=jnp.float32)
    sigmoid_gate = jax.nn.sigmoid(gate_pre)
    activated = (gate_pre * sigmoid_gate * up_pre).astype(jnp.bfloat16)
    summand = contract_last(activated, down_weights)
    results = summand.astype(jnp.bfloat16)
    results, arrived_grads, gate_up_weights = lax.optimization_barrier(
        (results, arrived_grads, gate_up_weights)
    )
    back_out = lax.all_to_all(results, "expert", split_axis=0, concat_axis=0, tiled=True)
    grad_act = jnp.dot(arrived_grads, down_weights, preferred_element_type=jnp.float32)
    grad_gate = (grad_act * up_pre * sigmoid_gate * (1.0 + gate_pre * (1.0 - sigmoid_gate))).astype(
        jnp.bfloat16
    )
    grad_up = (grad_act * gate_pre * sigmoid_gate).astype(jnp.bfloat16)
    gate_up = jnp.stack(
        [grad_gate.reshape(rows, 2, half), grad_up.reshape(rows, 2, half)], 2
    ).reshape(rows, 4 * half)
    row_grads = contract_last(gate_up, gate_up_weights).astype(jnp.bfloat16)
    gate_up_grads = contract_rows(inputs, gate_up)
    down_grads = contract_rows(arrived_grads, activated)
    row_grads, back_out, gate_up_grads, down_grads = lax.optimization_barrier(
        (row_grads, back_out, gate_up_grads, down_grads)
    )
    gate_up_grads = lax.psum_scatter(gate_up_grads, "dp", scatter_dimension=1, tiled=True)
    down_grads = lax.psum_scatter(down_grads, "dp", scatter_dimension=1, tiled=True)
    width = gate_up_grads.shape[0]
    weight_grads = jnp.concatenate(
        [gate_up_grads.reshape(width, 2, half).transpose(1, 0, 2), down_grads[None]], 0
    )[None].astype(jnp.bfloat16)
    back_grads = lax.all_to_all(row_grads, "expert", split_axis=0, concat_axis=0, tiled=True)
    back_grads, weight_grads = lax.optimization_barrier((back_grads, weight_grads))
    combined = scaled_rows(slot_gate, back_out).astype(jnp.bfloat16)
    products = contract_last(grad_out, back_out)
    gate_grads = jnp.sum(jnp.where(hit, products[:, None, :], 0.0), axis=2)
    token_grads = contract_rows(back_grads, select_slots).T.astype(jnp.bfloat16)
    return (combined, gate_grads, token_grads, weight_grads)


def solution(mesh):
    placed = (
        P(("dp", "expert"), None),
        P(("dp", "expert"), None),
        P(("dp", "expert"), None),
        P(("dp", "expert"), None),
        P(("dp", "expert"), None),
        P("expert", None, None, "dp"),
    )
    return jax.shard_map(
        local,
        mesh=mesh,
        in_specs=placed,
        out_specs=(
            P(("dp", "expert"), None),
            P(("dp", "expert"), None),
            P(("dp", "expert"), None),
            P("expert", None, None, "dp"),
        ),
        check_vma=False,
    )
```

```python
import jax
import jax.numpy as jnp
from jax import lax
from jax.sharding import PartitionSpec as P


def contract_rows(left, right):
    return lax.dot_general(
        left, right, (((0,), (0,)), ((), ())), preferred_element_type=jnp.float32
    )


def contract_last(left, right):
    return lax.dot_general(
        left, right, (((1,), (1,)), ((), ())), preferred_element_type=jnp.float32
    )


def split3(x):
    hi = x.astype(jnp.bfloat16)
    rest = x - hi.astype(jnp.float32)
    mid = rest.astype(jnp.bfloat16)
    lo = (rest - mid.astype(jnp.float32)).astype(jnp.bfloat16)
    return hi, mid, lo


def scaled_rows(weights, rows):
    hi, mid, lo = split3(weights)
    dot = lambda w: jnp.dot(w, rows, preferred_element_type=jnp.float32)
    return dot(hi) + dot(mid) + dot(lo)


def scaled_cols(weights, rows):
    hi, mid, lo = split3(weights)
    return contract_rows(hi, rows) + contract_rows(mid, rows) + contract_rows(lo, rows)


def local(tokens, gates, expert_ids, slots, grad_out, expert_weights):
    n_expert = lax.axis_size("expert")
    tok_count, top_count = expert_ids.shape
    capacity = tok_count * top_count // n_expert
    slot_rows = n_expert * capacity
    target = jnp.where(slots >= 0, expert_ids * capacity + slots, slot_rows)
    slot_ids = jnp.arange(slot_rows, dtype=jnp.int32)
    hit = target[:, :, None] == slot_ids[None, None, :]
    select = jnp.sum(hit.astype(jnp.float32), axis=1)
    slot_gate = jnp.sum(jnp.where(hit, gates[:, :, None], 0.0), axis=1)
    select_bf = select.astype(jnp.bfloat16)
    select_slots = sum(
        (target[:, k][None, :] == slot_ids[:, None]).astype(jnp.float32) for k in range(top_count)
    ).astype(jnp.bfloat16)
    send_tokens = jnp.dot(select_slots, tokens, preferred_element_type=jnp.float32).astype(
        jnp.bfloat16
    )
    send_grads = scaled_cols(slot_gate, grad_out).astype(jnp.bfloat16)
    arrived_tokens = lax.all_to_all(send_tokens, "expert", split_axis=0, concat_axis=0, tiled=True)
    arrived_tokens, send_grads, expert_weights = lax.optimization_barrier(
        (arrived_tokens, send_grads, expert_weights)
    )
    arrived_grads = lax.all_to_all(send_grads, "expert", split_axis=0, concat_axis=0, tiled=True)
    mine = expert_weights[0]
    other = lax.ppermute(mine, "dp", [(0, 1), (1, 0)])
    half = mine.shape[2]
    gate_weights = jnp.concatenate([mine[0], other[0]], 1)
    up_weights = jnp.concatenate([mine[1], other[1]], 1)
    gate_up_weights = jnp.concatenate([mine[0], mine[1], other[0], other[1]], 1)
    down_weights = jnp.concatenate([mine[2], other[2]], 1)
    inputs = arrived_tokens
    rows = inputs.shape[0]
    gate_pre = jnp.dot(inputs, gate_weights, preferred_element_type=jnp.float32)
    up_pre = jnp.dot(inputs, up_weights, preferred_element_type=jnp.float32)
    sigmoid_gate = jax.nn.sigmoid(gate_pre)
    activated = (gate_pre * sigmoid_gate * up_pre).astype(jnp.bfloat16)
    summand = contract_last(activated, down_weights)
    results = summand.astype(jnp.bfloat16)
    results, arrived_grads, gate_up_weights, down_weights, activated = lax.optimization_barrier(
        (results, arrived_grads, gate_up_weights, down_weights, activated)
    )
    back_out = lax.all_to_all(results, "expert", split_axis=0, concat_axis=0, tiled=True)
    grad_act = jnp.dot(arrived_grads, down_weights, preferred_element_type=jnp.float32)
    grad_gate = (grad_act * up_pre * sigmoid_gate * (1.0 + gate_pre * (1.0 - sigmoid_gate))).astype(
        jnp.bfloat16
    )
    grad_up = (grad_act * gate_pre * sigmoid_gate).astype(jnp.bfloat16)
    gate_up = jnp.stack(
        [grad_gate.reshape(rows, 2, half), grad_up.reshape(rows, 2, half)], 2
    ).reshape(rows, 4 * half)
    row_grads = contract_last(gate_up, gate_up_weights).astype(jnp.bfloat16)
    gate_up_grads = contract_rows(inputs, gate_up)
    down_grads = contract_rows(arrived_grads, activated)
    row_grads, back_out, gate_up_grads, down_grads = lax.optimization_barrier(
        (row_grads, back_out, gate_up_grads, down_grads)
    )
    swap = lambda x: lax.ppermute(x, "dp", [(0, 1), (1, 0)])
    gate_up_grads = gate_up_grads[:, : 2 * half] + swap(gate_up_grads[:, 2 * half :])
    down_grads = down_grads[:, :half] + swap(down_grads[:, half:])
    weight_grads = jnp.stack(
        [gate_up_grads[:, :half], gate_up_grads[:, half:], down_grads]
    )[None].astype(jnp.bfloat16)
    back_grads = lax.all_to_all(row_grads, "expert", split_axis=0, concat_axis=0, tiled=True)
    back_grads, weight_grads = lax.optimization_barrier((back_grads, weight_grads))
    combined = scaled_rows(slot_gate, back_out).astype(jnp.bfloat16)
    products = contract_last(grad_out, back_out)
    gate_grads = jnp.sum(jnp.where(hit, products[:, None, :], 0.0), axis=2)
    token_grads = contract_rows(back_grads, select_slots).T.astype(jnp.bfloat16)
    return (combined, gate_grads, token_grads, weight_grads)


def solution(mesh):
    placed = (
        P(("dp", "expert"), None),
        P(("dp", "expert"), None),
        P(("dp", "expert"), None),
        P(("dp", "expert"), None),
        P(("dp", "expert"), None),
        P("expert", None, None, "dp"),
    )
    return jax.shard_map(
        local,
        mesh=mesh,
        in_specs=placed,
        out_specs=(
            P(("dp", "expert"), None),
            P(("dp", "expert"), None),
            P(("dp", "expert"), None),
            P("expert", None, None, "dp"),
        ),
        check_vma=False,
    )
```

```python
import jax
import jax.numpy as jnp
from jax import lax
from jax.sharding import PartitionSpec as P


def contract_rows(left, right):
    return lax.dot_general(
        left, right, (((0,), (0,)), ((), ())), preferred_element_type=jnp.float32
    )


def contract_last(left, right):
    return lax.dot_general(
        left, right, (((1,), (1,)), ((), ())), preferred_element_type=jnp.float32
    )


def split3(x):
    hi = x.astype(jnp.bfloat16)
    rest = x - hi.astype(jnp.float32)
    mid = rest.astype(jnp.bfloat16)
    lo = (rest - mid.astype(jnp.float32)).astype(jnp.bfloat16)
    return hi, mid, lo


def scaled_rows(weights, rows):
    hi, mid, lo = split3(weights)
    dot = lambda w: jnp.dot(w, rows, preferred_element_type=jnp.float32)
    return dot(hi) + dot(mid) + dot(lo)


def scaled_cols(weights, rows):
    hi, mid, lo = split3(weights)
    return contract_rows(hi, rows) + contract_rows(mid, rows) + contract_rows(lo, rows)


def local(tokens, gates, expert_ids, slots, grad_out, expert_weights):
    n_expert = lax.axis_size("expert")
    tok_count, top_count = expert_ids.shape
    capacity = tok_count * top_count // n_expert
    slot_rows = n_expert * capacity
    target = jnp.where(slots >= 0, expert_ids * capacity + slots, slot_rows)
    slot_ids = jnp.arange(slot_rows, dtype=jnp.int32)
    hit = target[:, :, None] == slot_ids[None, None, :]
    select = jnp.sum(hit.astype(jnp.float32), axis=1)
    slot_gate = jnp.sum(jnp.where(hit, gates[:, :, None], 0.0), axis=1)
    select_bf = select.astype(jnp.bfloat16)
    select_slots = sum(
        (target[:, k][None, :] == slot_ids[:, None]).astype(jnp.float32) for k in range(top_count)
    ).astype(jnp.bfloat16)
    send_tokens = jnp.dot(select_slots, tokens, preferred_element_type=jnp.float32).astype(
        jnp.bfloat16
    )
    send_grads = scaled_cols(slot_gate, grad_out).astype(jnp.bfloat16)
    arrived_tokens = lax.all_to_all(send_tokens, "expert", split_axis=0, concat_axis=0, tiled=True)
    arrived_tokens, send_grads = lax.optimization_barrier((arrived_tokens, send_grads))
    arrived_grads = lax.all_to_all(send_grads, "expert", split_axis=0, concat_axis=0, tiled=True)
    mine = expert_weights[0]
    other = lax.ppermute(mine, "dp", [(0, 1), (1, 0)])
    half = mine.shape[2]
    gate_weights = jnp.concatenate([mine[0], other[0]], 1)
    up_weights = jnp.concatenate([mine[1], other[1]], 1)
    gate_up_weights = jnp.concatenate([mine[0], mine[1], other[0], other[1]], 1)
    down_weights = jnp.concatenate([mine[2], other[2]], 1)
    inputs = arrived_tokens
    rows = inputs.shape[0]
    gate_pre = jnp.dot(inputs, gate_weights, preferred_element_type=jnp.float32)
    up_pre = jnp.dot(inputs, up_weights, preferred_element_type=jnp.float32)
    sigmoid_gate = jax.nn.sigmoid(gate_pre)
    activated = (gate_pre * sigmoid_gate * up_pre).astype(jnp.bfloat16)
    summand = contract_last(activated, down_weights)
    results = summand.astype(jnp.bfloat16)
    results, arrived_grads, gate_up_weights, down_weights, activated = lax.optimization_barrier(
        (results, arrived_grads, gate_up_weights, down_weights, activated)
    )
    back_out = lax.all_to_all(results, "expert", split_axis=0, concat_axis=0, tiled=True)
    grad_act = jnp.dot(arrived_grads, down_weights, preferred_element_type=jnp.float32)
    grad_gate = (grad_act * up_pre * sigmoid_gate * (1.0 + gate_pre * (1.0 - sigmoid_gate))).astype(
        jnp.bfloat16
    )
    grad_up = (grad_act * gate_pre * sigmoid_gate).astype(jnp.bfloat16)
    gate_up = jnp.stack(
        [grad_gate.reshape(rows, 2, half), grad_up.reshape(rows, 2, half)], 2
    ).reshape(rows, 4 * half)
    row_grads = contract_last(gate_up, gate_up_weights).astype(jnp.bfloat16)
    gate_up_mine = contract_rows(gate_up[:, : 2 * half], inputs)
    gate_up_other = contract_rows(gate_up[:, 2 * half :], inputs)
    down_mine = contract_rows(activated[:, :half], arrived_grads)
    down_other = contract_rows(activated[:, half:], arrived_grads)
    row_grads, back_out, gate_up_mine, gate_up_other, down_mine, down_other = (
        lax.optimization_barrier(
            (row_grads, back_out, gate_up_mine, gate_up_other, down_mine, down_other)
        )
    )
    swap = lambda x: lax.ppermute(x, "dp", [(0, 1), (1, 0)])
    gate_up_grads = gate_up_mine + swap(gate_up_other)
    down_grads = down_mine + swap(down_other)
    weight_grads = jnp.concatenate(
        [gate_up_grads.reshape(2, half, -1), down_grads[None]], 0
    ).transpose(0, 2, 1)[None].astype(jnp.bfloat16)
    back_grads = lax.all_to_all(row_grads, "expert", split_axis=0, concat_axis=0, tiled=True)
    back_grads, weight_grads = lax.optimization_barrier((back_grads, weight_grads))
    combined = scaled_rows(slot_gate, back_out).astype(jnp.bfloat16)
    products = contract_last(grad_out, back_out)
    gate_grads = jnp.sum(jnp.where(hit, products[:, None, :], 0.0), axis=2)
    token_grads = contract_rows(back_grads, select_slots).T.astype(jnp.bfloat16)
    return (combined, gate_grads, token_grads, weight_grads)


def solution(mesh):
    placed = (
        P(("dp", "expert"), None),
        P(("dp", "expert"), None),
        P(("dp", "expert"), None),
        P(("dp", "expert"), None),
        P(("dp", "expert"), None),
        P("expert", None, None, "dp"),
    )
    return jax.shard_map(
        local,
        mesh=mesh,
        in_specs=placed,
        out_specs=(
            P(("dp", "expert"), None),
            P(("dp", "expert"), None),
            P(("dp", "expert"), None),
            P("expert", None, None, "dp"),
        ),
        check_vma=False,
    )
```

```python
import jax
import jax.numpy as jnp
from jax import lax
from jax.sharding import PartitionSpec as P


def contract_rows(left, right):
    return lax.dot_general(
        left, right, (((0,), (0,)), ((), ())), preferred_element_type=jnp.float32
    )


def contract_last(left, right):
    return lax.dot_general(
        left, right, (((1,), (1,)), ((), ())), preferred_element_type=jnp.float32
    )


def split3(x):
    hi = x.astype(jnp.bfloat16)
    rest = x - hi.astype(jnp.float32)
    mid = rest.astype(jnp.bfloat16)
    lo = (rest - mid.astype(jnp.float32)).astype(jnp.bfloat16)
    return hi, mid, lo


def scaled_rows(weights, rows):
    hi, mid, lo = split3(weights)
    dot = lambda w: jnp.dot(w, rows, preferred_element_type=jnp.float32)
    return dot(hi) + dot(mid) + dot(lo)


def scaled_cols(weights, rows):
    hi, mid, lo = split3(weights)
    return contract_rows(hi, rows) + contract_rows(mid, rows) + contract_rows(lo, rows)


def local(tokens, gates, expert_ids, slots, grad_out, expert_weights):
    n_expert = lax.axis_size("expert")
    tok_count, top_count = expert_ids.shape
    capacity = tok_count * top_count // n_expert
    slot_rows = n_expert * capacity
    target = jnp.where(slots >= 0, expert_ids * capacity + slots, slot_rows)
    slot_ids = jnp.arange(slot_rows, dtype=jnp.int32)
    hit = target[:, :, None] == slot_ids[None, None, :]
    select = jnp.sum(hit.astype(jnp.float32), axis=1)
    slot_gate = jnp.sum(jnp.where(hit, gates[:, :, None], 0.0), axis=1)
    select_bf = select.astype(jnp.bfloat16)
    select_slots = sum(
        (target[:, k][None, :] == slot_ids[:, None]).astype(jnp.float32) for k in range(top_count)
    ).astype(jnp.bfloat16)
    select_slots = lax.optimization_barrier(select_slots)
    send_tokens = jnp.dot(select_slots, tokens, preferred_element_type=jnp.float32).astype(
        jnp.bfloat16
    )
    send_grads = scaled_cols(slot_gate, grad_out).astype(jnp.bfloat16)
    arrived_tokens = lax.all_to_all(send_tokens, "expert", split_axis=0, concat_axis=0, tiled=True)
    arrived_tokens, send_grads, expert_weights = lax.optimization_barrier(
        (arrived_tokens, send_grads, expert_weights)
    )
    arrived_grads = lax.all_to_all(send_grads, "expert", split_axis=0, concat_axis=0, tiled=True)
    weights = lax.all_gather(expert_weights, "dp", axis=3, tiled=True)[0]
    half = expert_weights.shape[3]
    gate_up_weights = jnp.concatenate(
        [weights[0, :, :half], weights[1, :, :half], weights[0, :, half:], weights[1, :, half:]], 1
    )
    down_weights = weights[2]
    inputs = arrived_tokens
    rows = inputs.shape[0]
    gate_pre = jnp.dot(inputs, weights[0], preferred_element_type=jnp.float32)
    up_pre = jnp.dot(inputs, weights[1], preferred_element_type=jnp.float32)
    sigmoid_gate = jax.nn.sigmoid(gate_pre)
    activated = (gate_pre * sigmoid_gate * up_pre).astype(jnp.bfloat16)
    summand = contract_last(activated, down_weights)
    results = summand.astype(jnp.bfloat16)
    results, arrived_grads, gate_up_weights = lax.optimization_barrier(
        (results, arrived_grads, gate_up_weights)
    )
    back_out = lax.all_to_all(results, "expert", split_axis=0, concat_axis=0, tiled=True)
    grad_act = jnp.dot(arrived_grads, down_weights, preferred_element_type=jnp.float32)
    grad_gate = (grad_act * up_pre * sigmoid_gate * (1.0 + gate_pre * (1.0 - sigmoid_gate))).astype(
        jnp.bfloat16
    )
    grad_up = (grad_act * gate_pre * sigmoid_gate).astype(jnp.bfloat16)
    gate_up = jnp.stack(
        [grad_gate.reshape(rows, 2, half), grad_up.reshape(rows, 2, half)], 2
    ).reshape(rows, 4 * half)
    row_grads = contract_last(gate_up, gate_up_weights).astype(jnp.bfloat16)
    gate_up_grads = contract_rows(inputs, gate_up)
    down_grads = contract_rows(arrived_grads, activated)
    row_grads, back_out, gate_up_grads, down_grads = lax.optimization_barrier(
        (row_grads, back_out, gate_up_grads, down_grads)
    )
    gate_up_grads = lax.psum_scatter(gate_up_grads, "dp", scatter_dimension=1, tiled=True)
    down_grads = lax.psum_scatter(down_grads, "dp", scatter_dimension=1, tiled=True)
    width = gate_up_grads.shape[0]
    weight_grads = jnp.concatenate(
        [gate_up_grads.reshape(width, 2, half).transpose(1, 0, 2), down_grads[None]], 0
    )[None].astype(jnp.bfloat16)
    back_grads = lax.all_to_all(row_grads, "expert", split_axis=0, concat_axis=0, tiled=True)
    back_grads, weight_grads = lax.optimization_barrier((back_grads, weight_grads))
    combined = scaled_rows(slot_gate, back_out).astype(jnp.bfloat16)
    products = contract_last(grad_out, back_out)
    gate_grads = jnp.sum(jnp.where(hit, products[:, None, :], 0.0), axis=2)
    token_grads = jnp.dot(select_bf, back_grads, preferred_element_type=jnp.float32).astype(
        jnp.bfloat16
    )
    return (combined, gate_grads, token_grads, weight_grads)


def solution(mesh):
    placed = (
        P(("dp", "expert"), None),
        P(("dp", "expert"), None),
        P(("dp", "expert"), None),
        P(("dp", "expert"), None),
        P(("dp", "expert"), None),
        P("expert", None, None, "dp"),
    )
    return jax.shard_map(
        local,
        mesh=mesh,
        in_specs=placed,
        out_specs=(
            P(("dp", "expert"), None),
            P(("dp", "expert"), None),
            P(("dp", "expert"), None),
            P("expert", None, None, "dp"),
        ),
        check_vma=False,
    )
```

```python
import jax
import jax.numpy as jnp
from jax import lax
from jax.sharding import PartitionSpec as P


def contract_rows(left, right):
    return lax.dot_general(
        left, right, (((0,), (0,)), ((), ())), preferred_element_type=jnp.float32
    )


def contract_last(left, right):
    return lax.dot_general(
        left, right, (((1,), (1,)), ((), ())), preferred_element_type=jnp.float32
    )


def split3(x):
    hi = x.astype(jnp.bfloat16)
    rest = x - hi.astype(jnp.float32)
    mid = rest.astype(jnp.bfloat16)
    lo = (rest - mid.astype(jnp.float32)).astype(jnp.bfloat16)
    return hi, mid, lo


def scaled_rows(weights, rows):
    hi, mid, lo = split3(weights)
    dot = lambda w: jnp.dot(w, rows, preferred_element_type=jnp.float32)
    return dot(hi) + dot(mid) + dot(lo)


def scaled_cols(weights, rows):
    hi, mid, lo = split3(weights)
    return contract_rows(hi, rows) + contract_rows(mid, rows) + contract_rows(lo, rows)


def local(tokens, gates, expert_ids, slots, grad_out, expert_weights):
    n_expert = lax.axis_size("expert")
    tok_count, top_count = expert_ids.shape
    capacity = tok_count * top_count // n_expert
    slot_rows = n_expert * capacity
    target = jnp.where(slots >= 0, expert_ids * capacity + slots, slot_rows)
    slot_ids = jnp.arange(slot_rows, dtype=jnp.int32)
    hit = target[:, :, None] == slot_ids[None, None, :]
    select = jnp.sum(hit.astype(jnp.float32), axis=1)
    slot_gate = jnp.sum(jnp.where(hit, gates[:, :, None], 0.0), axis=1)
    select_bf = select.astype(jnp.bfloat16)
    select_slots = sum(
        (target[:, k][None, :] == slot_ids[:, None]).astype(jnp.float32) for k in range(top_count)
    ).astype(jnp.bfloat16)
    select_slots = lax.optimization_barrier(select_slots)
    send_tokens = jnp.dot(select_slots, tokens, preferred_element_type=jnp.bfloat16)
    send_grads = scaled_cols(slot_gate, grad_out).astype(jnp.bfloat16)
    arrived_tokens = lax.all_to_all(send_tokens, "expert", split_axis=0, concat_axis=0, tiled=True)
    arrived_tokens, send_grads, expert_weights = lax.optimization_barrier(
        (arrived_tokens, send_grads, expert_weights)
    )
    arrived_grads = lax.all_to_all(send_grads, "expert", split_axis=0, concat_axis=0, tiled=True)
    weights = lax.all_gather(expert_weights, "dp", axis=3, tiled=True)[0]
    half = expert_weights.shape[3]
    gate_up_weights = jnp.concatenate(
        [weights[0, :, :half], weights[1, :, :half], weights[0, :, half:], weights[1, :, half:]], 1
    )
    down_weights = weights[2]
    inputs = arrived_tokens
    rows = inputs.shape[0]
    gate_pre = jnp.dot(inputs, weights[0], preferred_element_type=jnp.float32)
    up_pre = jnp.dot(inputs, weights[1], preferred_element_type=jnp.float32)
    sigmoid_gate = jax.nn.sigmoid(gate_pre)
    activated = (gate_pre * sigmoid_gate * up_pre).astype(jnp.bfloat16)
    summand = contract_last(activated, down_weights)
    results = summand.astype(jnp.bfloat16)
    results, arrived_grads, gate_up_weights = lax.optimization_barrier(
        (results, arrived_grads, gate_up_weights)
    )
    back_out = lax.all_to_all(results, "expert", split_axis=0, concat_axis=0, tiled=True)
    grad_act = jnp.dot(arrived_grads, down_weights, preferred_element_type=jnp.float32)
    grad_gate = (grad_act * up_pre * sigmoid_gate * (1.0 + gate_pre * (1.0 - sigmoid_gate))).astype(
        jnp.bfloat16
    )
    grad_up = (grad_act * gate_pre * sigmoid_gate).astype(jnp.bfloat16)
    gate_up = jnp.stack(
        [grad_gate.reshape(rows, 2, half), grad_up.reshape(rows, 2, half)], 2
    ).reshape(rows, 4 * half)
    row_grads = contract_last(gate_up, gate_up_weights).astype(jnp.bfloat16)
    gate_up_grads = contract_rows(inputs, gate_up)
    down_grads = contract_rows(arrived_grads, activated)
    row_grads, back_out, gate_up_grads, down_grads = lax.optimization_barrier(
        (row_grads, back_out, gate_up_grads, down_grads)
    )
    gate_up_grads = lax.psum_scatter(gate_up_grads, "dp", scatter_dimension=1, tiled=True)
    down_grads = lax.psum_scatter(down_grads, "dp", scatter_dimension=1, tiled=True)
    width = gate_up_grads.shape[0]
    weight_grads = jnp.concatenate(
        [gate_up_grads.reshape(width, 2, half).transpose(1, 0, 2), down_grads[None]], 0
    )[None].astype(jnp.bfloat16)
    back_grads = lax.all_to_all(row_grads, "expert", split_axis=0, concat_axis=0, tiled=True)
    back_grads, weight_grads = lax.optimization_barrier((back_grads, weight_grads))
    combined = scaled_rows(slot_gate, back_out).astype(jnp.bfloat16)
    products = contract_last(grad_out, back_out)
    gate_grads = jnp.sum(jnp.where(hit, products[:, None, :], 0.0), axis=2)
    token_grads = jnp.dot(select_bf, back_grads, preferred_element_type=jnp.bfloat16)
    return (combined, gate_grads, token_grads, weight_grads)


def solution(mesh):
    placed = (
        P(("dp", "expert"), None),
        P(("dp", "expert"), None),
        P(("dp", "expert"), None),
        P(("dp", "expert"), None),
        P(("dp", "expert"), None),
        P("expert", None, None, "dp"),
    )
    return jax.shard_map(
        local,
        mesh=mesh,
        in_specs=placed,
        out_specs=(
            P(("dp", "expert"), None),
            P(("dp", "expert"), None),
            P(("dp", "expert"), None),
            P("expert", None, None, "dp"),
        ),
        check_vma=False,
    )
```

```python
import jax
import jax.numpy as jnp
from jax import lax
from jax.sharding import PartitionSpec as P


def contract_rows(left, right):
    return lax.dot_general(
        left, right, (((0,), (0,)), ((), ())), preferred_element_type=jnp.float32
    )


def contract_last(left, right):
    return lax.dot_general(
        left, right, (((1,), (1,)), ((), ())), preferred_element_type=jnp.float32
    )


def split3(x):
    hi = x.astype(jnp.bfloat16)
    rest = x - hi.astype(jnp.float32)
    mid = rest.astype(jnp.bfloat16)
    lo = (rest - mid.astype(jnp.float32)).astype(jnp.bfloat16)
    return hi, mid, lo


def scaled_rows(weights, rows):
    hi, mid, lo = split3(weights)
    dot = lambda w: jnp.dot(w, rows, preferred_element_type=jnp.float32)
    return dot(hi) + dot(mid) + dot(lo)


def scaled_cols(weights, rows):
    hi, mid, lo = split3(weights)
    return contract_rows(hi, rows) + contract_rows(mid, rows) + contract_rows(lo, rows)


def local(tokens, gates, expert_ids, slots, grad_out, expert_weights):
    n_expert = lax.axis_size("expert")
    tok_count, top_count = expert_ids.shape
    capacity = tok_count * top_count // n_expert
    slot_rows = n_expert * capacity
    target = jnp.where(slots >= 0, expert_ids * capacity + slots, slot_rows)
    slot_ids = jnp.arange(slot_rows, dtype=jnp.int32)
    hit = target[:, :, None] == slot_ids[None, None, :]
    select = jnp.sum(hit.astype(jnp.float32), axis=1)
    slot_gate = jnp.sum(jnp.where(hit, gates[:, :, None], 0.0), axis=1)
    select_bf = select.astype(jnp.bfloat16)
    select_slots = sum(
        (target[:, k][None, :] == slot_ids[:, None]).astype(jnp.float32) for k in range(top_count)
    ).astype(jnp.bfloat16)
    select_slots = lax.optimization_barrier(select_slots)
    send_tokens = jnp.dot(select_slots, tokens, preferred_element_type=jnp.bfloat16)
    gate_parts = jnp.concatenate(split3(slot_gate), 0)
    send_grads = contract_rows(gate_parts, jnp.concatenate([grad_out] * 3, 0)).astype(jnp.bfloat16)
    arrived_tokens = lax.all_to_all(send_tokens, "expert", split_axis=0, concat_axis=0, tiled=True)
    arrived_tokens, send_grads, expert_weights = lax.optimization_barrier(
        (arrived_tokens, send_grads, expert_weights)
    )
    arrived_grads = lax.all_to_all(send_grads, "expert", split_axis=0, concat_axis=0, tiled=True)
    weights = lax.all_gather(expert_weights, "dp", axis=3, tiled=True)[0]
    half = expert_weights.shape[3]
    gate_up_weights = jnp.concatenate(
        [weights[0, :, :half], weights[1, :, :half], weights[0, :, half:], weights[1, :, half:]], 1
    )
    down_weights = weights[2]
    inputs = arrived_tokens
    rows = inputs.shape[0]
    gate_pre = jnp.dot(inputs, weights[0], preferred_element_type=jnp.float32)
    up_pre = jnp.dot(inputs, weights[1], preferred_element_type=jnp.float32)
    sigmoid_gate = jax.nn.sigmoid(gate_pre)
    activated = (gate_pre * sigmoid_gate * up_pre).astype(jnp.bfloat16)
    summand = contract_last(activated, down_weights)
    results = summand.astype(jnp.bfloat16)
    results, arrived_grads, gate_up_weights = lax.optimization_barrier(
        (results, arrived_grads, gate_up_weights)
    )
    back_out = lax.all_to_all(results, "expert", split_axis=0, concat_axis=0, tiled=True)
    grad_act = jnp.dot(arrived_grads, down_weights, preferred_element_type=jnp.float32)
    grad_gate = (grad_act * up_pre * sigmoid_gate * (1.0 + gate_pre * (1.0 - sigmoid_gate))).astype(
        jnp.bfloat16
    )
    grad_up = (grad_act * gate_pre * sigmoid_gate).astype(jnp.bfloat16)
    gate_up = jnp.stack(
        [grad_gate.reshape(rows, 2, half), grad_up.reshape(rows, 2, half)], 2
    ).reshape(rows, 4 * half)
    row_grads = contract_last(gate_up, gate_up_weights).astype(jnp.bfloat16)
    gate_up_grads = contract_rows(inputs, gate_up)
    down_grads = contract_rows(arrived_grads, activated)
    row_grads, back_out, gate_up_grads, down_grads = lax.optimization_barrier(
        (row_grads, back_out, gate_up_grads, down_grads)
    )
    gate_up_grads = lax.psum_scatter(gate_up_grads, "dp", scatter_dimension=1, tiled=True)
    down_grads = lax.psum_scatter(down_grads, "dp", scatter_dimension=1, tiled=True)
    width = gate_up_grads.shape[0]
    weight_grads = jnp.concatenate(
        [gate_up_grads.reshape(width, 2, half).transpose(1, 0, 2), down_grads[None]], 0
    )[None].astype(jnp.bfloat16)
    back_grads = lax.all_to_all(row_grads, "expert", split_axis=0, concat_axis=0, tiled=True)
    back_grads, weight_grads = lax.optimization_barrier((back_grads, weight_grads))
    combined = scaled_rows(slot_gate, back_out).astype(jnp.bfloat16)
    products = contract_last(grad_out, back_out)
    gate_grads = jnp.sum(jnp.where(hit, products[:, None, :], 0.0), axis=2)
    token_grads = jnp.dot(select_bf, back_grads, preferred_element_type=jnp.bfloat16)
    return (combined, gate_grads, token_grads, weight_grads)


def solution(mesh):
    placed = (
        P(("dp", "expert"), None),
        P(("dp", "expert"), None),
        P(("dp", "expert"), None),
        P(("dp", "expert"), None),
        P(("dp", "expert"), None),
        P("expert", None, None, "dp"),
    )
    return jax.shard_map(
        local,
        mesh=mesh,
        in_specs=placed,
        out_specs=(
            P(("dp", "expert"), None),
            P(("dp", "expert"), None),
            P(("dp", "expert"), None),
            P("expert", None, None, "dp"),
        ),
        check_vma=False,
    )
```

```python
import jax
import jax.numpy as jnp
from jax import lax
from jax.sharding import PartitionSpec as P


def contract_rows(left, right):
    return lax.dot_general(
        left, right, (((0,), (0,)), ((), ())), preferred_element_type=jnp.float32
    )


def contract_last(left, right):
    return lax.dot_general(
        left, right, (((1,), (1,)), ((), ())), preferred_element_type=jnp.float32
    )


def split3(x):
    hi = x.astype(jnp.bfloat16)
    rest = x - hi.astype(jnp.float32)
    mid = rest.astype(jnp.bfloat16)
    lo = (rest - mid.astype(jnp.float32)).astype(jnp.bfloat16)
    return hi, mid, lo


def scaled_rows(weights, rows):
    hi, mid, lo = split3(weights)
    dot = lambda w: jnp.dot(w, rows, preferred_element_type=jnp.float32)
    return dot(hi) + dot(mid) + dot(lo)


def scaled_cols(weights, rows):
    hi, mid, lo = split3(weights)
    return contract_rows(hi, rows) + contract_rows(mid, rows) + contract_rows(lo, rows)


def local(tokens, gates, expert_ids, slots, grad_out, expert_weights):
    n_expert = lax.axis_size("expert")
    tok_count, top_count = expert_ids.shape
    capacity = tok_count * top_count // n_expert
    slot_rows = n_expert * capacity
    target = jnp.where(slots >= 0, expert_ids * capacity + slots, slot_rows)
    slot_ids = jnp.arange(slot_rows, dtype=jnp.int32)
    hit = target[:, :, None] == slot_ids[None, None, :]
    select = jnp.sum(hit.astype(jnp.float32), axis=1)
    slot_gate = jnp.sum(jnp.where(hit, gates[:, :, None], 0.0), axis=1)
    select_bf = select.astype(jnp.bfloat16)
    select_slots = sum(
        (target[:, k][None, :] == slot_ids[:, None]).astype(jnp.float32) for k in range(top_count)
    ).astype(jnp.bfloat16)
    select_slots = lax.optimization_barrier(select_slots)
    send_tokens = jnp.dot(select_slots, tokens, preferred_element_type=jnp.bfloat16)
    gate_parts = jnp.concatenate(split3(slot_gate), 0)
    send_grads = contract_rows(gate_parts, jnp.concatenate([grad_out] * 3, 0)).astype(jnp.bfloat16)
    arrived_tokens = lax.all_to_all(send_tokens, "expert", split_axis=0, concat_axis=0, tiled=True)
    arrived_tokens, send_grads, expert_weights = lax.optimization_barrier(
        (arrived_tokens, send_grads, expert_weights)
    )
    arrived_grads = lax.all_to_all(send_grads, "expert", split_axis=0, concat_axis=0, tiled=True)
    weights = lax.all_gather(expert_weights, "dp", axis=3, tiled=True)[0]
    half = expert_weights.shape[3]
    gate_up_weights = jnp.concatenate(
        [weights[0, :, :half], weights[1, :, :half], weights[0, :, half:], weights[1, :, half:]], 1
    )
    down_weights = weights[2]
    inputs = arrived_tokens
    rows = inputs.shape[0]
    gate_pre = jnp.dot(inputs, weights[0], preferred_element_type=jnp.float32)
    up_pre = jnp.dot(inputs, weights[1], preferred_element_type=jnp.float32)
    sigmoid_gate = jax.nn.sigmoid(gate_pre)
    activated = (gate_pre * sigmoid_gate * up_pre).astype(jnp.bfloat16)
    summand = contract_last(activated, down_weights)
    results = summand.astype(jnp.bfloat16)
    results, arrived_grads, gate_up_weights = lax.optimization_barrier(
        (results, arrived_grads, gate_up_weights)
    )
    back_out = lax.all_to_all(results, "expert", split_axis=0, concat_axis=0, tiled=True)
    grad_act = jnp.dot(arrived_grads, down_weights, preferred_element_type=jnp.float32)
    grad_gate = (grad_act * up_pre * sigmoid_gate * (1.0 + gate_pre * (1.0 - sigmoid_gate))).astype(
        jnp.bfloat16
    )
    grad_up = (grad_act * gate_pre * sigmoid_gate).astype(jnp.bfloat16)
    gate_up = jnp.stack(
        [grad_gate.reshape(rows, 2, half), grad_up.reshape(rows, 2, half)], 2
    ).reshape(rows, 4 * half)
    row_grads = contract_last(gate_up, gate_up_weights).astype(jnp.bfloat16)
    gate_up_grads = contract_rows(inputs, gate_up)
    down_grads = contract_rows(arrived_grads, activated)
    row_grads, back_out, gate_up_grads, down_grads = lax.optimization_barrier(
        (row_grads, back_out, gate_up_grads, down_grads)
    )
    gate_up_grads = lax.psum_scatter(gate_up_grads, "dp", scatter_dimension=1, tiled=True)
    down_grads = lax.psum_scatter(down_grads, "dp", scatter_dimension=1, tiled=True)
    width = gate_up_grads.shape[0]
    weight_grads = jnp.concatenate(
        [gate_up_grads.reshape(width, 2, half).transpose(1, 0, 2), down_grads[None]], 0
    )[None].astype(jnp.bfloat16)
    back_grads = lax.all_to_all(row_grads, "expert", split_axis=0, concat_axis=0, tiled=True)
    back_grads, weight_grads = lax.optimization_barrier((back_grads, weight_grads))
    tok = slot_gate.shape[0]
    parts = jnp.dot(jnp.concatenate(split3(slot_gate), 0), back_out, preferred_element_type=jnp.float32)
    combined = (parts[:tok] + parts[tok : 2 * tok] + parts[2 * tok :]).astype(jnp.bfloat16)
    products = contract_last(grad_out, back_out)
    gate_grads = jnp.sum(jnp.where(hit, products[:, None, :], 0.0), axis=2)
    token_grads = jnp.dot(select_bf, back_grads, preferred_element_type=jnp.bfloat16)
    return (combined, gate_grads, token_grads, weight_grads)


def solution(mesh):
    placed = (
        P(("dp", "expert"), None),
        P(("dp", "expert"), None),
        P(("dp", "expert"), None),
        P(("dp", "expert"), None),
        P(("dp", "expert"), None),
        P("expert", None, None, "dp"),
    )
    return jax.shard_map(
        local,
        mesh=mesh,
        in_specs=placed,
        out_specs=(
            P(("dp", "expert"), None),
            P(("dp", "expert"), None),
            P(("dp", "expert"), None),
            P("expert", None, None, "dp"),
        ),
        check_vma=False,
    )
```

```python
import jax
import jax.numpy as jnp
from jax import lax
from jax.sharding import PartitionSpec as P


def contract_rows(left, right):
    return lax.dot_general(
        left, right, (((0,), (0,)), ((), ())), preferred_element_type=jnp.float32
    )


def contract_last(left, right):
    return lax.dot_general(
        left, right, (((1,), (1,)), ((), ())), preferred_element_type=jnp.float32
    )


def split3(x):
    hi = x.astype(jnp.bfloat16)
    rest = x - hi.astype(jnp.float32)
    mid = rest.astype(jnp.bfloat16)
    lo = (rest - mid.astype(jnp.float32)).astype(jnp.bfloat16)
    return hi, mid, lo


def scaled_rows(weights, rows):
    hi, mid, lo = split3(weights)
    dot = lambda w: jnp.dot(w, rows, preferred_element_type=jnp.float32)
    return dot(hi) + dot(mid) + dot(lo)


def scaled_cols(weights, rows):
    hi, mid, lo = split3(weights)
    return contract_rows(hi, rows) + contract_rows(mid, rows) + contract_rows(lo, rows)


def local(tokens, gates, expert_ids, slots, grad_out, expert_weights):
    n_expert = lax.axis_size("expert")
    tok_count, top_count = expert_ids.shape
    capacity = tok_count * top_count // n_expert
    slot_rows = n_expert * capacity
    target = jnp.where(slots >= 0, expert_ids * capacity + slots, slot_rows)
    slot_ids = jnp.arange(slot_rows, dtype=jnp.int32)
    hit = target[:, :, None] == slot_ids[None, None, :]
    select = jnp.sum(hit.astype(jnp.float32), axis=1)
    slot_gate = jnp.sum(jnp.where(hit, gates[:, :, None], 0.0), axis=1)
    select_bf = select.astype(jnp.bfloat16)
    select_slots = sum(
        (target[:, k][None, :] == slot_ids[:, None]).astype(jnp.float32) for k in range(top_count)
    ).astype(jnp.bfloat16)
    select_slots = lax.optimization_barrier(select_slots)
    pad = tok_count % 256 and 256 - tok_count % 256
    send_tokens = jnp.dot(
        jnp.pad(select_slots, ((0, 0), (0, pad))),
        jnp.pad(tokens, ((0, pad), (0, 0))),
        preferred_element_type=jnp.bfloat16,
    )
    gate_parts = jnp.concatenate(split3(slot_gate), 0)
    send_grads = contract_rows(gate_parts, jnp.concatenate([grad_out] * 3, 0)).astype(jnp.bfloat16)
    arrived_tokens = lax.all_to_all(send_tokens, "expert", split_axis=0, concat_axis=0, tiled=True)
    arrived_tokens, send_grads, expert_weights = lax.optimization_barrier(
        (arrived_tokens, send_grads, expert_weights)
    )
    arrived_grads = lax.all_to_all(send_grads, "expert", split_axis=0, concat_axis=0, tiled=True)
    weights = lax.all_gather(expert_weights, "dp", axis=3, tiled=True)[0]
    half = expert_weights.shape[3]
    gate_up_weights = jnp.concatenate(
        [weights[0, :, :half], weights[1, :, :half], weights[0, :, half:], weights[1, :, half:]], 1
    )
    down_weights = weights[2]
    inputs = arrived_tokens
    rows = inputs.shape[0]
    gate_pre = jnp.dot(inputs, weights[0], preferred_element_type=jnp.float32)
    up_pre = jnp.dot(inputs, weights[1], preferred_element_type=jnp.float32)
    sigmoid_gate = jax.nn.sigmoid(gate_pre)
    activated = (gate_pre * sigmoid_gate * up_pre).astype(jnp.bfloat16)
    summand = contract_last(activated, down_weights)
    results = summand.astype(jnp.bfloat16)
    results, arrived_grads, gate_up_weights = lax.optimization_barrier(
        (results, arrived_grads, gate_up_weights)
    )
    back_out = lax.all_to_all(results, "expert", split_axis=0, concat_axis=0, tiled=True)
    grad_act = jnp.dot(arrived_grads, down_weights, preferred_element_type=jnp.float32)
    grad_gate = (grad_act * up_pre * sigmoid_gate * (1.0 + gate_pre * (1.0 - sigmoid_gate))).astype(
        jnp.bfloat16
    )
    grad_up = (grad_act * gate_pre * sigmoid_gate).astype(jnp.bfloat16)
    gate_up = jnp.stack(
        [grad_gate.reshape(rows, 2, half), grad_up.reshape(rows, 2, half)], 2
    ).reshape(rows, 4 * half)
    row_grads = contract_last(gate_up, gate_up_weights).astype(jnp.bfloat16)
    gate_up_grads = contract_rows(inputs, gate_up)
    down_grads = contract_rows(arrived_grads, activated)
    row_grads, back_out, gate_up_grads, down_grads = lax.optimization_barrier(
        (row_grads, back_out, gate_up_grads, down_grads)
    )
    gate_up_grads = lax.psum_scatter(gate_up_grads, "dp", scatter_dimension=1, tiled=True)
    down_grads = lax.psum_scatter(down_grads, "dp", scatter_dimension=1, tiled=True)
    width = gate_up_grads.shape[0]
    weight_grads = jnp.concatenate(
        [gate_up_grads.reshape(width, 2, half).transpose(1, 0, 2), down_grads[None]], 0
    )[None].astype(jnp.bfloat16)
    back_grads = lax.all_to_all(row_grads, "expert", split_axis=0, concat_axis=0, tiled=True)
    back_grads, weight_grads = lax.optimization_barrier((back_grads, weight_grads))
    tok = slot_gate.shape[0]
    parts = jnp.dot(jnp.concatenate(split3(slot_gate), 0), back_out, preferred_element_type=jnp.float32)
    combined = (parts[:tok] + parts[tok : 2 * tok] + parts[2 * tok :]).astype(jnp.bfloat16)
    products = contract_last(grad_out, back_out)
    gate_grads = jnp.sum(jnp.where(hit, products[:, None, :], 0.0), axis=2)
    token_grads = jnp.dot(select_bf, back_grads, preferred_element_type=jnp.bfloat16)
    return (combined, gate_grads, token_grads, weight_grads)


def solution(mesh):
    placed = (
        P(("dp", "expert"), None),
        P(("dp", "expert"), None),
        P(("dp", "expert"), None),
        P(("dp", "expert"), None),
        P(("dp", "expert"), None),
        P("expert", None, None, "dp"),
    )
    return jax.shard_map(
        local,
        mesh=mesh,
        in_specs=placed,
        out_specs=(
            P(("dp", "expert"), None),
            P(("dp", "expert"), None),
            P(("dp", "expert"), None),
            P("expert", None, None, "dp"),
        ),
        check_vma=False,
    )
```

```python
import jax
import jax.numpy as jnp
from jax import lax
from jax.sharding import PartitionSpec as P


def contract_rows(left, right):
    return lax.dot_general(
        left, right, (((0,), (0,)), ((), ())), preferred_element_type=jnp.float32
    )


def contract_last(left, right):
    return lax.dot_general(
        left, right, (((1,), (1,)), ((), ())), preferred_element_type=jnp.float32
    )


def split3(x):
    hi = x.astype(jnp.bfloat16)
    rest = x - hi.astype(jnp.float32)
    mid = rest.astype(jnp.bfloat16)
    lo = (rest - mid.astype(jnp.float32)).astype(jnp.bfloat16)
    return hi, mid, lo


def scaled_rows(weights, rows):
    hi, mid, lo = split3(weights)
    dot = lambda w: jnp.dot(w, rows, preferred_element_type=jnp.float32)
    return dot(hi) + dot(mid) + dot(lo)


def scaled_cols(weights, rows):
    hi, mid, lo = split3(weights)
    return contract_rows(hi, rows) + contract_rows(mid, rows) + contract_rows(lo, rows)


def local(tokens, gates, expert_ids, slots, grad_out, expert_weights):
    n_expert = lax.axis_size("expert")
    tok_count, top_count = expert_ids.shape
    capacity = tok_count * top_count // n_expert
    slot_rows = n_expert * capacity
    target = jnp.where(slots >= 0, expert_ids * capacity + slots, slot_rows)
    slot_ids = jnp.arange(slot_rows, dtype=jnp.int32)
    hit = target[:, :, None] == slot_ids[None, None, :]
    select = jnp.sum(hit.astype(jnp.float32), axis=1)
    slot_gate = jnp.sum(jnp.where(hit, gates[:, :, None], 0.0), axis=1)
    select_bf = select.astype(jnp.bfloat16)
    select_slots = sum(
        (target[:, k][None, :] == slot_ids[:, None]).astype(jnp.float32) for k in range(top_count)
    ).astype(jnp.bfloat16)
    send_tokens = jnp.dot(select_slots, tokens, preferred_element_type=jnp.bfloat16)
    gate_parts = jnp.concatenate(split3(slot_gate), 0)
    send_grads = contract_rows(gate_parts, jnp.concatenate([grad_out] * 3, 0)).astype(jnp.bfloat16)
    arrived_tokens = lax.all_to_all(send_tokens, "expert", split_axis=0, concat_axis=0, tiled=True)
    arrived_tokens, send_grads, expert_weights = lax.optimization_barrier(
        (arrived_tokens, send_grads, expert_weights)
    )
    arrived_grads = lax.all_to_all(send_grads, "expert", split_axis=0, concat_axis=0, tiled=True)
    weights = lax.all_gather(expert_weights, "dp", axis=3, tiled=True)[0]
    half = expert_weights.shape[3]
    gate_up_weights = jnp.concatenate(
        [weights[0, :, :half], weights[1, :, :half], weights[0, :, half:], weights[1, :, half:]], 1
    )
    down_weights = weights[2]
    inputs = arrived_tokens
    rows = inputs.shape[0]
    gate_pre = jnp.dot(inputs, weights[0], preferred_element_type=jnp.float32)
    up_pre = jnp.dot(inputs, weights[1], preferred_element_type=jnp.float32)
    sigmoid_gate = jax.nn.sigmoid(gate_pre)
    activated = (gate_pre * sigmoid_gate * up_pre).astype(jnp.bfloat16)
    summand = contract_last(activated, down_weights)
    results = summand.astype(jnp.bfloat16)
    results, arrived_grads, gate_up_weights = lax.optimization_barrier(
        (results, arrived_grads, gate_up_weights)
    )
    back_out = lax.all_to_all(results, "expert", split_axis=0, concat_axis=0, tiled=True)
    grad_act = jnp.dot(arrived_grads, down_weights, preferred_element_type=jnp.float32)
    grad_gate = (grad_act * up_pre * sigmoid_gate * (1.0 + gate_pre * (1.0 - sigmoid_gate))).astype(
        jnp.bfloat16
    )
    grad_up = (grad_act * gate_pre * sigmoid_gate).astype(jnp.bfloat16)
    gate_up = jnp.stack(
        [grad_gate.reshape(rows, 2, half), grad_up.reshape(rows, 2, half)], 2
    ).reshape(rows, 4 * half)
    row_grads = contract_last(gate_up, gate_up_weights).astype(jnp.bfloat16)
    gate_up_grads = contract_rows(inputs, gate_up)
    down_grads = contract_rows(arrived_grads, activated)
    row_grads, back_out, gate_up_grads, down_grads = lax.optimization_barrier(
        (row_grads, back_out, gate_up_grads, down_grads)
    )
    gate_up_grads = lax.psum_scatter(gate_up_grads, "dp", scatter_dimension=1, tiled=True)
    down_grads = lax.psum_scatter(down_grads, "dp", scatter_dimension=1, tiled=True)
    width = gate_up_grads.shape[0]
    weight_grads = jnp.concatenate(
        [gate_up_grads.reshape(width, 2, half).transpose(1, 0, 2), down_grads[None]], 0
    )[None].astype(jnp.bfloat16)
    back_grads = lax.all_to_all(row_grads, "expert", split_axis=0, concat_axis=0, tiled=True)
    back_grads, weight_grads = lax.optimization_barrier((back_grads, weight_grads))
    tok = slot_gate.shape[0]
    parts = jnp.dot(jnp.concatenate(split3(slot_gate), 0), back_out, preferred_element_type=jnp.float32)
    combined = (parts[:tok] + parts[tok : 2 * tok] + parts[2 * tok :]).astype(jnp.bfloat16)
    products = contract_last(grad_out, back_out)
    gate_grads = jnp.sum(jnp.where(hit, products[:, None, :], 0.0), axis=2)
    token_grads = jnp.dot(select_bf, back_grads, preferred_element_type=jnp.bfloat16)
    return (combined, gate_grads, token_grads, weight_grads)


def solution(mesh):
    placed = (
        P(("dp", "expert"), None),
        P(("dp", "expert"), None),
        P(("dp", "expert"), None),
        P(("dp", "expert"), None),
        P(("dp", "expert"), None),
        P("expert", None, None, "dp"),
    )
    return jax.shard_map(
        local,
        mesh=mesh,
        in_specs=placed,
        out_specs=(
            P(("dp", "expert"), None),
            P(("dp", "expert"), None),
            P(("dp", "expert"), None),
            P("expert", None, None, "dp"),
        ),
        check_vma=False,
    )
```

```python
import jax
import jax.numpy as jnp
from jax import lax
from jax.sharding import PartitionSpec as P


def contract_rows(left, right):
    return lax.dot_general(
        left, right, (((0,), (0,)), ((), ())), preferred_element_type=jnp.float32
    )


def contract_last(left, right):
    return lax.dot_general(
        left, right, (((1,), (1,)), ((), ())), preferred_element_type=jnp.float32
    )


def split3(x):
    hi = x.astype(jnp.bfloat16)
    rest = x - hi.astype(jnp.float32)
    mid = rest.astype(jnp.bfloat16)
    lo = (rest - mid.astype(jnp.float32)).astype(jnp.bfloat16)
    return hi, mid, lo


def scaled_rows(weights, rows):
    hi, mid, lo = split3(weights)
    dot = lambda w: jnp.dot(w, rows, preferred_element_type=jnp.float32)
    return dot(hi) + dot(mid) + dot(lo)


def scaled_cols(weights, rows):
    hi, mid, lo = split3(weights)
    return contract_rows(hi, rows) + contract_rows(mid, rows) + contract_rows(lo, rows)


def local(tokens, gates, expert_ids, slots, grad_out, expert_weights):
    n_expert = lax.axis_size("expert")
    tok_count, top_count = expert_ids.shape
    capacity = tok_count * top_count // n_expert
    slot_rows = n_expert * capacity
    target = jnp.where(slots >= 0, expert_ids * capacity + slots, slot_rows)
    slot_ids = jnp.arange(slot_rows, dtype=jnp.int32)
    hit = target[:, :, None] == slot_ids[None, None, :]
    select = jnp.sum(hit.astype(jnp.float32), axis=1)
    slot_gate = jnp.sum(jnp.where(hit, gates[:, :, None], 0.0), axis=1)
    select_bf = select.astype(jnp.bfloat16)
    select_slots = sum(
        (target[:, k][None, :] == slot_ids[:, None]).astype(jnp.float32) for k in range(top_count)
    ).astype(jnp.bfloat16)
    send_tokens = jnp.dot(select_slots, tokens, preferred_element_type=jnp.bfloat16)
    gate_parts = jnp.concatenate(split3(slot_gate), 0)
    send_grads = contract_rows(gate_parts, jnp.concatenate([grad_out] * 3, 0)).astype(jnp.bfloat16)
    arrived_tokens = lax.all_to_all(send_tokens, "expert", split_axis=0, concat_axis=0, tiled=True)
    arrived_tokens, send_grads, expert_weights = lax.optimization_barrier(
        (arrived_tokens, send_grads, expert_weights)
    )
    arrived_grads = lax.all_to_all(send_grads, "expert", split_axis=0, concat_axis=0, tiled=True)
    weights = lax.all_gather(expert_weights, "dp", axis=3, tiled=True)[0]
    half = expert_weights.shape[3]
    gate_up_weights = jnp.concatenate(
        [weights[0, :, :half], weights[1, :, :half], weights[0, :, half:], weights[1, :, half:]], 1
    )
    down_weights = weights[2]
    inputs = arrived_tokens
    rows = inputs.shape[0]
    gate_pre = jnp.dot(inputs, weights[0], preferred_element_type=jnp.float32)
    up_pre = jnp.dot(inputs, weights[1], preferred_element_type=jnp.float32)
    sigmoid_gate = jax.nn.sigmoid(gate_pre)
    activated = (gate_pre * sigmoid_gate * up_pre).astype(jnp.bfloat16)
    summand = contract_last(activated, down_weights)
    results = summand.astype(jnp.bfloat16)
    results, arrived_grads, gate_up_weights = lax.optimization_barrier(
        (results, arrived_grads, gate_up_weights)
    )
    back_out = lax.all_to_all(results, "expert", split_axis=0, concat_axis=0, tiled=True)
    grad_act = jnp.dot(arrived_grads, down_weights, preferred_element_type=jnp.float32)
    grad_gate = (grad_act * up_pre * sigmoid_gate * (1.0 + gate_pre * (1.0 - sigmoid_gate))).astype(
        jnp.bfloat16
    )
    grad_up = (grad_act * gate_pre * sigmoid_gate).astype(jnp.bfloat16)
    gate_up = jnp.stack(
        [grad_gate.reshape(rows, 2, half), grad_up.reshape(rows, 2, half)], 2
    ).reshape(rows, 4 * half)
    row_grads = contract_last(gate_up, gate_up_weights).astype(jnp.bfloat16)
    gate_up_grads = contract_rows(inputs, gate_up)
    down_grads = contract_rows(arrived_grads, activated)
    row_grads, back_out, gate_up_grads, down_grads = lax.optimization_barrier(
        (row_grads, back_out, gate_up_grads, down_grads)
    )
    gate_up_grads = lax.psum_scatter(gate_up_grads, "dp", scatter_dimension=1, tiled=True)
    down_grads = lax.psum_scatter(down_grads, "dp", scatter_dimension=1, tiled=True)
    width = gate_up_grads.shape[0]
    weight_grads = jnp.concatenate(
        [gate_up_grads.reshape(width, 2, half).transpose(1, 0, 2), down_grads[None]], 0
    )[None].astype(jnp.bfloat16)
    back_grads = lax.all_to_all(row_grads, "expert", split_axis=0, concat_axis=0, tiled=True)
    back_grads, weight_grads = lax.optimization_barrier((back_grads, weight_grads))
    tok = slot_gate.shape[0]
    parts = jnp.dot(jnp.concatenate(split3(slot_gate), 0), back_out, preferred_element_type=jnp.float32)
    combined = (parts[:tok] + parts[tok : 2 * tok] + parts[2 * tok :]).astype(jnp.bfloat16)
    products = contract_last(grad_out, back_out)
    gate_grads = jnp.sum(jnp.where(hit, products[:, None, :], 0.0), axis=2)
    select_tokens = sum(
        (target[:, k][:, None] == slot_ids[None, :]).astype(jnp.float32) for k in range(top_count)
    ).astype(jnp.bfloat16)
    token_grads = jnp.dot(select_tokens, back_grads, preferred_element_type=jnp.bfloat16)
    return (combined, gate_grads, token_grads, weight_grads)


def solution(mesh):
    placed = (
        P(("dp", "expert"), None),
        P(("dp", "expert"), None),
        P(("dp", "expert"), None),
        P(("dp", "expert"), None),
        P(("dp", "expert"), None),
        P("expert", None, None, "dp"),
    )
    return jax.shard_map(
        local,
        mesh=mesh,
        in_specs=placed,
        out_specs=(
            P(("dp", "expert"), None),
            P(("dp", "expert"), None),
            P(("dp", "expert"), None),
            P("expert", None, None, "dp"),
        ),
        check_vma=False,
    )
```
